32 devices in a mesh: dp: 8 (over z, x), tensor: 4 (over y, core).
Axes of the slice: x: 2, y: 2, z: 4, core: 2. Of those that a mesh axis runs over, the one named last changes fastest.
Arguments:
- queries: bfloat16 [8192, 1024], P('dp', 'tensor')
- keys: bfloat16 [8192, 1024], P('dp', 'tensor')
- values: bfloat16 [8192, 1024], P('dp', 'tensor'), may hold values from -6 to 6
- mem_keys: bfloat16 [16384, 1024], P('dp', 'tensor')
- mem_values: bfloat16 [16384, 1024], P('dp', 'tensor'), may hold values from -6 to 6
- gate_bias: float32 [8], P('tensor'), may hold values from -3 to 3
- out_weight: bfloat16 [1024, 7168], P('tensor'), may hold values from -0.25 to 0.25
- retrieved: int32 [64, 4], P('dp'), may hold values from 0 to 127, as said below
- block_slot: int32 [128], replicated, may hold values from 0 to 127, as said below
Outputs:
- mixed: bfloat16 [7168, 8192], P('tensor', 'dp')
The draws below stay inside these ranges and needn't reach their ends.
Inputs may be any that keep to these rules, and one draw needn't show every extreme that they name: Row b lists the 4 memory blocks retrieved for query block b, all different. Among the 32 entries of the rows of one device, at most 8 name blocks whose slots lie on one device (slot // 16), and these name at most 4 different blocks. `block_slot`: each slot once.
All inputs are finite; a program needn't handle non-finite values.
Results may differ from the reference program's by a relative error of at most 0.014.
Values may be sent and summed in bfloat16 or wider, within the bound.
A program may use at most 128 MiB of HBM per device.

```python
import jax
import jax.numpy as jnp
from jax import lax

D = 7168
HEAD = 128
HEADS_DEV = 2
BLOCK = 128
SEG = 512
TOPK = 4
REQ_CAP = 8
UNIQ_CAP = 4
TOK_DEV = 1024
MB_DEV = 16
TOKENS = 8192
QB_DEV = 8
NQB = 64
MEMBLOCKS = 128
MEMTOK = 16384
HEADS = 8
HD = 1024


def relabel(labels, first_value, second_value):
    return jnp.where(labels == first_value, second_value, jnp.where(labels == second_value, first_value, labels)).astype(jnp.int32)


def request_plan(key):
    base_key = jax.random.fold_in(key, 4101)
    subkeys = jax.random.split(base_key, 6)
    device_count = NQB // QB_DEV
    first_perm = jax.random.permutation(subkeys[0], MEMBLOCKS).astype(jnp.int32)
    block_at_slot = jnp.argsort(first_perm, stable=True).astype(jnp.int32)
    hot_owner = jax.random.randint(subkeys[1], (), 0, device_count).astype(jnp.int32)
    request_count = QB_DEV * TOPK
    rest_count = request_count - REQ_CAP
    other_owners = (hot_owner + 1 + jnp.arange(device_count - 1, dtype=jnp.int32)) % device_count
    owner_pool = jnp.repeat(other_owners, UNIQ_CAP)
    pool_length = (device_count - 1) * UNIQ_CAP
    shuffles = jax.vmap(lambda subkey: jax.random.permutation(subkey, pool_length))(jax.random.split(subkeys[2], device_count))
    picked_owners = owner_pool[shuffles[:, :rest_count]]
    owners = jnp.concatenate([jnp.full((device_count, REQ_CAP), hot_owner, jnp.int32), picked_owners.astype(jnp.int32)], axis=1)
    request_order = jnp.arange(request_count, dtype=jnp.int32)
    same_owner = owners[:, :, None] == owners[:, None, :]
    earlier = request_order[None, None, :] < request_order[None, :, None]
    owner_rank = jnp.sum(same_owner & earlier, axis=2).astype(jnp.int32)
    owner_rank = jnp.where(request_order[None, :] < REQ_CAP, request_order[None, :] // 2, owner_rank)
    spread = jax.random.randint(subkeys[3], (device_count, request_count), 0, MB_DEV // UNIQ_CAP).astype(jnp.int32)
    partner = jnp.where(request_order < REQ_CAP, request_order // 2 * 2, request_order)
    spread = spread[:, partner]
    local_slot = owner_rank + UNIQ_CAP * spread
    global_slot = owners * MB_DEV + local_slot
    first_label = block_at_slot[global_slot[0, 0]]
    block_at_slot = relabel(block_at_slot, first_label, 0)
    last_label = block_at_slot[global_slot[0, 2]]
    block_at_slot = relabel(block_at_slot, last_label, MEMBLOCKS - 1)
    slot_of_block = jnp.argsort(block_at_slot, stable=True).astype(jnp.int32)
    block_ids = block_at_slot[global_slot]
    block_perm = jax.vmap(lambda subkey: jax.random.permutation(subkey, QB_DEV))(jax.random.split(subkeys[4], device_count)).astype(jnp.int32)
    rotation = jax.random.randint(subkeys[5], (device_count, QB_DEV), 0, TOPK).astype(jnp.int32)
    query_block = block_perm[:, request_order % QB_DEV]
    column = (request_order[None, :] // QB_DEV + jnp.take_along_axis(rotation, query_block, axis=1)) % TOPK
    device_rows = jnp.broadcast_to(jnp.arange(device_count, dtype=jnp.int32)[:, None], (device_count, request_count))
    placed = jnp.zeros((device_count, QB_DEV, TOPK), jnp.int32).at[device_rows, query_block, column].set(block_ids)
    return (placed.reshape(NQB, TOPK), slot_of_block)


def draw_retrieved(key, part):
    return request_plan(key)[0]


def draw_block_slot(key, part):
    return request_plan(key)[1]


def draw_queries(key, part):
    base_rows = jax.random.normal(jax.random.fold_in(key, 11), (TOKENS, HD), jnp.float32)
    return base_rows.astype(jnp.bfloat16)


def draw_keys(key, part):
    base_rows = jax.random.normal(jax.random.fold_in(key, 31), (TOKENS, HD), jnp.float32)
    return base_rows.astype(jnp.bfloat16)


def draw_mem_keys(key, part):
    base_rows = jax.random.normal(jax.random.fold_in(key, 41), (MEMTOK, HD), jnp.float32)
    return base_rows.astype(jnp.bfloat16)


def raised(array, stream_key, source, target, blocks, factor):
    def block_of(position):
        return (jnp.arange(array.shape[position]) // (array.shape[position] // blocks)).reshape((-1,) + (1,) * (array.ndim - 1 - position))

    first = jax.random.permutation(stream_key, blocks)[block_of(target)]
    far = (block_of(target) + blocks // 2) % blocks
    return jnp.where((block_of(source) == first) | (block_of(source) == far), factor * array, array)


def levels(rng, dims, shards, least, high):
    factor_of = 1.0
    for dim, shards_of in shards:
        heights = jax.random.uniform(jax.random.fold_in(jax.random.fold_in(rng, 6), dim), (shards_of,), jnp.float32, least / len(shards), high / len(shards))
        factor_of = factor_of * jnp.repeat(jnp.exp(heights), dims[dim] // shards_of).reshape((-1,) + (1,) * (len(dims) - 1 - dim))
    return factor_of


def bell_draw(stream_key, extent, width, bound, cuts=(), kind=jnp.bfloat16):
    factor_of = levels(stream_key, extent, cuts, -0.22, 0.18) if cuts else 1.0
    values = jax.random.normal(stream_key, extent, jnp.float32) * width * factor_of
    return jnp.minimum(jnp.maximum(values, -bound), bound).astype(kind)


def gaussian_with(stream_key, shape, scale, most, pieces, heavy, kind=jnp.bfloat16):
    result = scale * jax.random.normal(stream_key, shape, jnp.float32)
    if pieces:
        result = result * levels(stream_key, shape, pieces, -0.22, 0.18)
    return jnp.clip(raised(result, jax.random.fold_in(stream_key, 3), *heavy), -most, most).astype(kind)


def setup_inputs(seed: int = 0) -> dict:
    splits = jax.random.split(jax.random.key(seed), 10)
    queries = draw_queries(jax.random.fold_in(splits[9], 71), 0)
    keys = draw_keys(jax.random.fold_in(splits[9], 71), 0)
    values = bell_draw(splits[2], (TOKENS, HD), 1.0, 6.0, ((0, 8), (1, 4)))
    mem_keys = draw_mem_keys(jax.random.fold_in(splits[9], 71), 0)
    mem_values = bell_draw(splits[4], (MEMTOK, HD), 1.0, 6.0, ((0, 8), (1, 4)))
    gate_bias = jnp.clip(jax.random.uniform(splits[5], (HEADS,), jnp.float32, -3.0, 3.0) * levels(splits[5], (HEADS,), ((0, 4),), -0.4, 0.0), -3.0, 3.0)
    out_weight = gaussian_with(splits[6], (HD, D), HD ** -0.5, 0.25, ((0, 4),), (0, 1, 4, 2.0))
    retrieved = draw_retrieved(jax.random.fold_in(splits[9], 71), 0)
    block_slot = draw_block_slot(jax.random.fold_in(splits[9], 71), 0)
    return {"queries": queries, "keys": keys, "values": values, "mem_keys": mem_keys, "mem_values": mem_values, "gate_bias": gate_bias, "out_weight": out_weight, "retrieved": retrieved, "block_slot": block_slot}


def attend(query_rows, key_rows, value_rows, causal):
    scores = jnp.einsum("qhd,khd->hqk", query_rows.astype(jnp.float32), key_rows.astype(jnp.float32)) * (HEAD ** -0.5)
    if causal:
        causal_mask = jnp.arange(query_rows.shape[0])[:, None] >= jnp.arange(key_rows.shape[0])[None, :]
        scores = jnp.where(causal_mask[None, :, :], scores, -jnp.inf)
    weights = jax.nn.softmax(scores, axis=-1).astype(jnp.bfloat16)
    return jnp.einsum("hqk,khd->qhd", weights.astype(jnp.float32), value_rows.astype(jnp.float32))


def reference(queries, keys, values, mem_keys, mem_values, gate_bias, out_weight, retrieved, block_slot):
    seg_count = TOKENS // SEG
    seg_shape = (seg_count, SEG, HEADS, HEAD)

    def local_segment(triple_rows):
        return attend(triple_rows[0], triple_rows[1], triple_rows[2], True)

    local_out = lax.map(local_segment, (queries.reshape(seg_shape), keys.reshape(seg_shape), values.reshape(seg_shape)))
    local_out = local_out.reshape(TOKENS, HEADS, HEAD)

    memory_keys = mem_keys.reshape(MEMBLOCKS, BLOCK, HEADS, HEAD)
    memory_values = mem_values.reshape(MEMBLOCKS, BLOCK, HEADS, HEAD)
    slot_lists = block_slot[retrieved].astype(jnp.int32)

    def memory_block(block_pair):
        query_rows, slot_row = block_pair
        key_rows = memory_keys[slot_row].reshape(TOPK * BLOCK, HEADS, HEAD)
        value_rows = memory_values[slot_row].reshape(TOPK * BLOCK, HEADS, HEAD)
        return attend(query_rows, key_rows, value_rows, False)

    mem_out = lax.map(memory_block, (queries.reshape(NQB, BLOCK, HEADS, HEAD), slot_lists))
    mem_out = mem_out.reshape(TOKENS, HEADS, HEAD)

    mem_gate = jax.nn.sigmoid(gate_bias.astype(jnp.float32))[None, :, None]
    attended = (mem_gate * mem_out + (1.0 - mem_gate) * local_out).astype(jnp.bfloat16).reshape(TOKENS, HD)

    group_count = HEADS // HEADS_DEV
    group_width = HEADS_DEV * HEAD
    weight_groups = out_weight.reshape(group_count, group_width, D)

    def project(token_rows):
        group_rows = token_rows.reshape(TOK_DEV, group_count, group_width).transpose(1, 0, 2)

        def add_group(running, group_pair):
            partial_value = jnp.dot(group_pair[0], group_pair[1], preferred_element_type=jnp.float32).astype(jnp.bfloat16)
            partial_value = lax.optimization_barrier(partial_value)
            return running + partial_value.astype(jnp.float32), None

        running, unused = lax.scan(add_group, jnp.zeros((TOK_DEV, D), jnp.float32), (group_rows, weight_groups))
        return running.astype(jnp.bfloat16)

    mixed = lax.map(project, attended.reshape(TOKENS // TOK_DEV, TOK_DEV, HD)).reshape(TOKENS, D)
    return mixed.T
```

```python
import functools
import math

import jax
import jax.numpy as jnp
from jax import lax
from jax.experimental import pallas as pl
from jax.experimental.pallas import tpu as pltpu
from jax.sharding import PartitionSpec as P

BLOCK = 128
SEG = 512
TOPK = 4
UNIQ_CAP = 4
CHUNK = 256
NEG = -3.0e38
MESH = pl.DeviceIdType.MESH
NT = (((1,), (1,)), ((), ()))
TN = (((0,), (0,)), ((), ()))
RANK_ROW = UNIQ_CAP
SLOT_ROW = UNIQ_CAP + 1


def flipped(index, mask):
    bit = 1
    result = index
    while bit <= mask:
        if mask & bit:
            result = result + bit * (1 - 2 * (lax.rem(lax.div(index, bit), 2)))
        bit *= 2
    return result


def at_least(value, bound):
    return lax.div(value - bound + 64, 64)


def layer_kernel(
    n, groups, heads, rung_minor, sliced,
    ret_ref, slot_ref, gate_ref, q_hbm, k_hbm, v_hbm, mk_hbm, mv_hbm, w_hbm,
    out_hbm,
    qb, kl, vl, vt, kown, vraw, vown, sk, sv, land_k, land_v, loc, po, st,
    o_out, s_out, o_in, s_in, wg, ag, out_vm, tab_in, tab_sm,
    in_sem, smem_sem, own_w_sem, out_sem, t_ss, t_rs, q_ss, q_rs, k_ss, k_rs, v_ss, v_rs,
    o_ss, o_rs, s_ss, s_rs, w_ss, w_rs, a_ss, a_rs, f_ss, f_rs,
):
    me = lax.axis_index("dp")
    tme = lax.axis_index("tensor")
    peers = 2 * n
    local_blocks = kown.shape[1]
    chunks, head = ag.shape[0], kl.shape[2]
    tok = kl.shape[1]
    feats = wg.shape[1]
    scale = head ** -0.5 * math.log2(math.e)

    def split(index):
        if rung_minor:
            return lax.div(index, 2), lax.rem(index, 2)
        return lax.rem(index, n), lax.div(index, n)

    def join(line, rung):
        return line * 2 + rung if rung_minor else rung * n + line

    z, x = split(me)
    mirror = join(z, 1 - x)
    half = lax.div(2 * z, n)
    near = z * (1 - half) + (n - 1 - z) * half

    def stage_flow(j):
        both = at_least(2 * near, j + 1)
        tau = both * (j // 2) + (1 - both) * (j - near)
        primary = both * (1 - j % 2) + (1 - both)
        right = primary * (1 - half) + (1 - primary) * half
        return right, right * (n - 1 - tau) + (1 - right) * tau

    loads = []

    def load(src, dst):
        copy = pltpu.make_async_copy(src, dst, in_sem.at[len(loads)])
        copy.start()
        loads.append(copy)

    def cols(h):
        return pl.ds(h * head, head)

    for h in range(heads):
        load(q_hbm.at[:, cols(h)], qb.at[z, h])
    for h in range(heads):
        load(mk_hbm.at[:, :, cols(h)], kown.at[h])
    load(mv_hbm, vraw)
    for h in range(heads):
        load(k_hbm.at[:, cols(h)], kl.at[h])
    load(v_hbm, vl)

    barrier = pltpu.get_barrier_semaphore()
    for m in range(1, peers):
        pl.semaphore_signal(barrier, inc=1, device_id={"dp": flipped(me, m)}, device_id_type=MESH)
    for m in range(1, groups):
        pl.semaphore_signal(
            barrier, inc=1, device_id={"tensor": flipped(tme, m)}, device_id_type=MESH
        )

    wide = tab_in.shape[2]
    lane = lax.broadcasted_iota(jnp.int32, (8, wide), 1)
    sub = lax.broadcasted_iota(jnp.int32, (8, wide), 0)
    inner = lax.rem(lane, local_blocks)
    slots = jnp.zeros((8, wide), jnp.int32)
    present = jnp.zeros((8, wide), jnp.int32)
    for b in range(tok // BLOCK):
        for i in range(TOPK):
            slot = slot_ref[ret_ref[i, b]]
            slots = jnp.where(lane == b * TOPK + i, slot, slots)
            present = jnp.where(lane == slot, 1, present)
    rank = present
    shift = 1
    while shift < local_blocks:
        rank = rank + jnp.where(inner >= shift, pltpu.roll(rank, shift, 1), 0)
        shift *= 2
    rank = rank - present
    wanted = jnp.where((present == 1) & (rank == sub), inner, 0)
    shift = local_blocks // 2
    while shift >= 1:
        wanted = jnp.maximum(wanted, pltpu.roll(wanted, wide - shift, 1))
        shift //= 2
    table = jnp.where(sub < UNIQ_CAP, wanted, jnp.where(sub == RANK_ROW, rank, slots))
    tab_in[me] = table

    pl.semaphore_wait(barrier, peers - 1 + groups - 1)

    tables = []
    for m in range(1, peers):
        copy = pltpu.make_async_remote_copy(
            src_ref=tab_in.at[me], dst_ref=tab_in.at[me], send_sem=t_ss.at[m],
            recv_sem=t_rs.at[m], device_id={"dp": flipped(me, m)}, device_id_type=MESH,
        )
        copy.start()
        tables.append(copy)

    def tokens(c):
        return pl.ds(pl.multiple_of(c * CHUNK, CHUNK), CHUNK)

    def q_copy(right, source, h, c):
        part = qb.at[source, h, tokens(c)]
        return pltpu.make_async_remote_copy(
            src_ref=part, dst_ref=part, send_sem=q_ss.at[right, source, h, c],
            recv_sem=q_rs.at[source, h, c],
            device_id={"dp": join(z + 2 * right - 1, x)}, device_id_type=MESH,
        )

    def leads(right):
        return z < n - 1 if right else z > 0

    def exists(right, k):
        return z >= k if right else z < n - k

    def q_own(h):
        for right in (1, 0):
            @pl.when(leads(right))
            def _():
                for c in range(chunks):
                    q_copy(right, z, h, c).start()

    def q_step(h, k, c):
        for right in (1, 0):
            source = z - k if right else z + k

            @pl.when(exists(right, k))
            def _():
                q_copy(right, source, h, c).wait_recv()
                if k < n - 1:
                    @pl.when(leads(right))
                    def _():
                        q_copy(right, source, h, c).start()

    def q_steps(h, k):
        def step(c, carry):
            q_step(h, k, c)
            return carry

        lax.fori_loop(0, chunks, step, 0)

    for h in range(heads):
        loads[h].wait()
    q_own(0)

    def weight_part(t):
        if sliced:
            return w_hbm.at[:, pl.ds(pl.multiple_of(t * feats, 128), feats)]
        return w_hbm.at[t]

    def group_rows(t):
        return pl.ds(pl.multiple_of(t * heads * head, 128), heads * head)

    w_copies = []
    for m in range(1, groups):
        peer = flipped(tme, m)
        copy = pltpu.make_async_remote_copy(
            src_ref=weight_part(peer), dst_ref=wg.at[group_rows(tme)],
            send_sem=w_ss.at[m], recv_sem=w_rs.at[m], device_id={"tensor": peer},
            device_id_type=MESH,
        )
        copy.start()
        w_copies.append(copy)
    own_w = pltpu.make_async_copy(weight_part(tme), wg.at[group_rows(tme)], own_w_sem)
    own_w.start()

    for h in range(heads):
        loads[heads + h].wait()
    loads[2 * heads].wait()

    def turn_values(i, carry):
        for h in range(heads):
            vown[h, i] = vraw[i, :, h * head:(h + 1) * head].T
        return carry

    lax.fori_loop(0, local_blocks, turn_values, 0)

    for copy in tables:
        copy.wait_recv()
    to_smem = pltpu.make_async_copy(tab_in, tab_sm, smem_sem)
    to_smem.start()
    to_smem.wait()

    ships = {}
    for h in range(heads):
        for j in range(n):
            d = z if j == n - 1 else stage_flow(j)[1]
            reader = join(d, 1 - x)
            for key, own, send, land, ss, rs in (
                ("k", kown, sk, land_k, k_ss, k_rs), ("v", vown, sv, land_v, v_ss, v_rs)
            ):
                for c in range(UNIQ_CAP):
                    send[h, j, c] = own[h, tab_sm[reader, c, me * local_blocks]]
                copy = pltpu.make_async_remote_copy(
                    src_ref=send.at[h, j], dst_ref=land[h][j].at[pl.ds(UNIQ_CAP, UNIQ_CAP)],
                    send_sem=ss.at[h, j], recv_sem=rs.at[h, j], device_id={"dp": mirror},
                    device_id_type=MESH,
                )
                copy.start()
                ships[key, h, j] = copy

    for copy in loads[2 * heads + 1:]:
        copy.wait()

    def turn_local(i, carry):
        rows = pl.ds(pl.multiple_of(i * BLOCK, BLOCK), BLOCK)
        for h in range(heads):
            vt[h, i] = vl[rows, h * head:(h + 1) * head].T
        return carry

    lax.fori_loop(0, tok // BLOCK, turn_local, 0)

    def gate(h, width):
        bias = jnp.full((1, width), gate_ref[h], jnp.float32)
        return 1.0 / (1.0 + jnp.exp(-bias))

    blocks_seg = SEG // BLOCK
    per_chunk = CHUNK // BLOCK

    def local_segment(u, carry):
        s, h = lax.div(u, heads), lax.rem(u, heads)
        first = s * blocks_seg
        key_row = lax.broadcasted_iota(jnp.int32, (BLOCK, BLOCK), 0)
        query_col = lax.broadcasted_iota(jnp.int32, (BLOCK, BLOCK), 1)
        keep = 1.0 - gate(h, BLOCK)
        for i in range(blocks_seg):
            span = (i + 1) * BLOCK
            base = pl.multiple_of(s * SEG, SEG)
            scores = lax.dot_general(
                kl[h, pl.ds(base, span)], qb[z, h, pl.ds(base + i * BLOCK, BLOCK)], NT,
                preferred_element_type=jnp.float32,
            )
            last = jnp.where(key_row <= query_col, scores[i * BLOCK:], -jnp.inf)
            scores = last if i == 0 else jnp.concatenate([scores[:i * BLOCK], last], axis=0)
            top = jnp.max(scores, axis=0, keepdims=True)
            weights = jnp.exp2((scores - top) * scale)
            total = jnp.sum(weights, axis=0, keepdims=True)
            vals = jnp.concatenate([vt[h, first + g] for g in range(i + 1)], axis=1)
            out = jnp.dot(
                vals, weights.astype(jnp.bfloat16), preferred_element_type=jnp.float32
            )
            loc[h, first + i] = out * (keep / total)
        q_step(0, 1, u)
        return carry

    lax.fori_loop(0, chunks, local_segment, 0)
    for k in range(2, n):
        q_steps(0, k)
    for h in range(1, heads):
        q_own(h)

    def partial_block(h, j, d, b):
        owner_at = join(d, x)
        places, valid = [], []
        for i in range(TOPK):
            slot = tab_sm[owner_at, SLOT_ROW, b * TOPK + i]
            line, rung = split(lax.div(slot, local_blocks))
            side = lax.rem(rung + x, 2)
            places.append(side * UNIQ_CAP + tab_sm[owner_at, RANK_ROW, slot])
            valid.append(line == z)
        keys = jnp.concatenate([land_k[h][j][p] for p in places], axis=0)
        rows = pl.ds(pl.multiple_of(b * BLOCK, BLOCK), BLOCK)
        scores = lax.dot_general(keys, qb[d, h, rows], NT, preferred_element_type=jnp.float32)
        scores = jnp.concatenate(
            [
                jnp.where(valid[i], scores[i * BLOCK:(i + 1) * BLOCK], NEG)
                for i in range(TOPK)
            ],
            axis=0,
        )
        top = jnp.max(scores, axis=0, keepdims=True)
        weights = jnp.exp2((scores - top) * scale)
        total = jnp.sum(weights, axis=0, keepdims=True)
        vals = jnp.concatenate([land_v[h][j][p] for p in places], axis=1)
        out = jnp.dot(vals, weights.astype(jnp.bfloat16), preferred_element_type=jnp.float32)
        return out, top, total

    def stat_rows(top, total):
        row = lax.broadcasted_iota(jnp.int32, (8, top.shape[1]), 0)
        return jnp.where(row == 0, top, total)

    def partial_chunk(h, j, d, c):
        for blk in range(per_chunk):
            out, top, total = partial_block(h, j, d, c * per_chunk + blk)
            at = slice(blk * BLOCK, (blk + 1) * BLOCK)
            po[:, at] = out
            st[:, at] = stat_rows(top, total)

    def merged(right, d, h, c):
        o_copy(right, d, h, 0, c).wait_recv()
        s_copy(right, d, h, 0, c).wait_recv()
        top, total = st[0:1], st[1:2]
        top_in, total_in = s_in[right, d, h, c, 0:1], s_in[right, d, h, c, 1:2]
        new = jnp.maximum(top, top_in)
        mine = jnp.exp2((top - new) * scale)
        theirs = jnp.exp2((top_in - new) * scale)
        out = po[...] * mine + o_in[right, d, h, c].astype(jnp.float32) * theirs
        return out, new, total * mine + total_in * theirs

    def o_copy(right, d, h, j, c):
        return pltpu.make_async_remote_copy(
            src_ref=o_out.at[h, j, c], dst_ref=o_in.at[right, d, h, c],
            send_sem=o_ss.at[h, j, c], recv_sem=o_rs.at[right, d, h, c],
            device_id={"dp": join(z + 2 * right - 1, x)}, device_id_type=MESH,
        )

    def s_copy(right, d, h, j, c):
        return pltpu.make_async_remote_copy(
            src_ref=s_out.at[h, j, c], dst_ref=s_in.at[right, d, h, c],
            send_sem=s_ss.at[h, j, c], recv_sem=s_rs.at[right, d, h, c],
            device_id={"dp": join(z + 2 * right - 1, x)}, device_id_type=MESH,
        )

    def head_rows(t, h):
        return pl.ds(pl.multiple_of(t * heads * head + h * head, 128), head)

    def a_copy(h, c, m):
        part = ag.at[c, head_rows(tme, h)]
        return pltpu.make_async_remote_copy(
            src_ref=part, dst_ref=part, send_sem=a_ss.at[h, c, m], recv_sem=a_rs.at[h, c, m],
            device_id={"tensor": flipped(tme, m)}, device_id_type=MESH,
        )

    def f_copy(h, c, m):
        part = ag.at[c, head_rows(flipped(tme, m), h)]
        return pltpu.make_async_remote_copy(
            src_ref=part, dst_ref=part, send_sem=f_ss.at[h, c, m], recv_sem=f_rs.at[h, c, m],
            device_id={"tensor": flipped(tme, 1)}, device_id_type=MESH,
        )

    others = list(range(2, groups, 2))

    def arrive(h, j, d):
        ships["k", h, j].wait_recv()
        ships["v", h, j].wait_recv()
        reader = join(d, x)
        for c in range(UNIQ_CAP):
            at = tab_sm[reader, c, me * local_blocks]
            land_k[h][j][c] = kown[h, at]
            land_v[h][j][c] = vown[h, at]

    def stage(h, j):
        right, d = stage_flow(j)
        arrive(h, j, d)
        starts = right * z + (1 - right) * (n - 1 - z) == 0

        def chunk(c, carry):
            partial_chunk(h, j, d, c)

            @pl.when(starts)
            def _():
                o_out[h, j, c] = po[...].astype(o_out.dtype)
                s_out[h, j, c] = st[...]

            @pl.when(jnp.logical_not(starts))
            def _():
                out, top, total = merged(right, d, h, c)
                o_out[h, j, c] = out.astype(o_out.dtype)
                s_out[h, j, c] = stat_rows(top, total)

            o_copy(right, d, h, j, c).start()
            s_copy(right, d, h, j, c).start()
            return carry

        lax.fori_loop(0, chunks, chunk, 0)

    def own_stage(h):
        j = n - 1
        arrive(h, j, z)

        def chunk(c, carry):
            partial_chunk(h, j, z, c)
            for right in (1, 0):
                @pl.when(exists(right, 1))
                def _():
                    out, top, total = merged(right, z, h, c)
                    po[...] = out
                    st[...] = stat_rows(top, total)

            local = jnp.concatenate(
                [loc[h, c * per_chunk + blk] for blk in range(per_chunk)], axis=1
            )
            result = po[...] * (gate(h, CHUNK) / st[1:2]) + local
            ag[c, head_rows(tme, h)] = result.astype(ag.dtype)
            for m in others + [1]:
                a_copy(h, c, m).start()
            return carry

        lax.fori_loop(0, chunks, chunk, 0)

    for h in range(heads):
        for j in range(n - 1):
            stage(h, j)
            if h + 1 < heads and j >= 1:
                q_steps(h + 1, j)
        own_stage(h)
        if h + 1 < heads:
            q_steps(h + 1, n - 1)

    def forward(h, c):
        for m in others:
            a_copy_from(h, c, m).wait_recv()
            f_copy(h, c, m).start()

    def a_copy_from(h, c, m):
        part = ag.at[c, head_rows(flipped(tme, m), h)]
        return pltpu.make_async_remote_copy(
            src_ref=part, dst_ref=part, send_sem=a_ss.at[h, c, m], recv_sem=a_rs.at[h, c, m],
            device_id={"tensor": flipped(tme, m)}, device_id_type=MESH,
        )

    def f_copy_from(h, c, m):
        part = ag.at[c, head_rows(flipped(flipped(tme, 1), m), h)]
        return pltpu.make_async_remote_copy(
            src_ref=part, dst_ref=part, send_sem=f_ss.at[h, c, m], recv_sem=f_rs.at[h, c, m],
            device_id={"tensor": flipped(tme, 1)}, device_id_type=MESH,
        )

    tile = 256 if feats % 256 == 0 else feats

    def out_copy(c):
        return pltpu.make_async_copy(out_vm.at[c], out_hbm.at[:, tokens(c)], out_sem.at[c])

    def settle(c):
        for h in range(heads):
            a_copy_from(h, c, 1).wait_recv()
            for m in others:
                f_copy_from(h, c, m).wait_recv()

    def project(c):
        def part(i, carry):
            at = pl.ds(pl.multiple_of(i * tile, tile), tile) if tile < feats else slice(None)
            out = lax.dot_general(wg[:, at], ag[c], TN, preferred_element_type=jnp.float32)
            out_vm[c, at, :] = out.astype(out_vm.dtype)
            return carry

        lax.fori_loop(0, feats // tile, part, 0)
        out_copy(c).start()

    def forward_all(h):
        def step(c, carry):
            forward(h, c)
            return carry

        lax.fori_loop(0, chunks, step, 0)

    for h in range(heads - 1):
        forward_all(h)
    for copy in w_copies:
        copy.wait()
    own_w.wait()
    forward(heads - 1, 0)

    def finish(c, carry):
        @pl.when(c < chunks - 1)
        def _():
            forward(heads - 1, c + 1)

        settle(c)
        project(c)
        return carry

    lax.fori_loop(0, chunks, finish, 0)

    for copy in tables:
        copy.wait_send()
    for copy in ships.values():
        copy.wait_send()

    def left(c, carry):
        for h in range(heads):
            for right in (1, 0):
                for k in range(0, n - 1):
                    source = z - k if right else z + k

                    @pl.when(jnp.logical_and(exists(right, k), leads(right)))
                    def _():
                        q_copy(right, source, h, c).wait_send()

            for j in range(n - 1):
                right, d = stage_flow(j)
                o_copy(right, d, h, j, c).wait_send()
                s_copy(right, d, h, j, c).wait_send()
            for m in others + [1]:
                a_copy(h, c, m).wait_send()
            for m in others:
                f_copy(h, c, m).wait_send()
        out_copy(c).wait()
        return carry

    lax.fori_loop(0, chunks, left, 0)


def shards(
    queries, keys, values, mem_keys, mem_values, gate_bias, out_weight, retrieved, block_slot
):
    tok, width = queries.shape
    heads = gate_bias.shape[0]
    head = width // heads
    peers = lax.axis_size("dp")
    groups = lax.axis_size("tensor")
    n = peers // 2
    local_blocks = mem_keys.shape[0] // BLOCK
    feats = out_weight.shape[1] // groups
    chunks = tok // CHUNK
    sliced = feats % 128 == 0
    weight = out_weight
    if not sliced:
        weight = out_weight.reshape(width, groups, feats).transpose(1, 0, 2)
    blocked = (local_blocks, BLOCK, width)
    bf16, f32 = jnp.bfloat16, jnp.float32
    landing = pltpu.VMEM((2 * UNIQ_CAP, BLOCK, head), bf16)
    landings = tuple(tuple(landing for _ in range(n)) for _ in range(heads))
    wide = block_slot.shape[0]
    dma = pltpu.SemaphoreType.DMA
    smem = pl.BlockSpec(memory_space=pltpu.SMEM)
    any_spec = pl.BlockSpec(memory_space=pltpu.HBM)
    return pl.pallas_call(
        functools.partial(layer_kernel, n, groups, heads, peers <= 8, sliced),
        out_shape=jax.ShapeDtypeStruct((feats, tok), bf16),
        in_specs=[smem] * 3 + [any_spec] * 6,
        out_specs=any_spec,
        scratch_shapes=[
            pltpu.VMEM((n, heads, tok, head), bf16),
            pltpu.VMEM((heads, tok, head), bf16),
            pltpu.VMEM((tok, width), bf16),
            pltpu.VMEM((heads, tok // BLOCK, head, BLOCK), bf16),
            pltpu.VMEM((heads, local_blocks, BLOCK, head), bf16),
            pltpu.VMEM(blocked, bf16),
            pltpu.VMEM((heads, local_blocks, head, BLOCK), bf16),
            pltpu.VMEM((heads, n, UNIQ_CAP, BLOCK, head), bf16),
            pltpu.VMEM((heads, n, UNIQ_CAP, head, BLOCK), bf16),
            landings,
            landings,
            pltpu.VMEM((heads, tok // BLOCK, head, BLOCK), f32),
            pltpu.VMEM((head, CHUNK), f32),
            pltpu.VMEM((8, CHUNK), f32),
            pltpu.VMEM((heads, n - 1, chunks, head, CHUNK), bf16),
            pltpu.VMEM((heads, n - 1, chunks, 8, CHUNK), f32),
            pltpu.VMEM((2, n, heads, chunks, head, CHUNK), bf16),
            pltpu.VMEM((2, n, heads, chunks, 8, CHUNK), f32),
            pltpu.VMEM((groups * width, feats), bf16),
            pltpu.VMEM((chunks, groups * width, CHUNK), bf16),
            pltpu.VMEM((chunks, feats, CHUNK), bf16),
            pltpu.VMEM((peers, 8, wide), jnp.int32),
            pltpu.SMEM((peers, 8, wide), jnp.int32),
            dma((3 * heads + 2,)),
            dma(()),
            dma(()),
            dma((chunks,)),
            dma((peers,)),
            dma((peers,)),
            dma((2, n, heads, chunks)),
            dma((n, heads, chunks)),
            dma((heads, n)),
            dma((heads, n)),
            dma((heads, n)),
            dma((heads, n)),
            dma((heads, n - 1, chunks)),
            dma((2, n, heads, chunks)),
            dma((heads, n - 1, chunks)),
            dma((2, n, heads, chunks)),
            dma((groups,)),
            dma((groups,)),
            dma((heads, chunks, groups)),
            dma((heads, chunks, groups)),
            dma((heads, chunks, groups)),
            dma((heads, chunks, groups)),
        ],
        compiler_params=pltpu.CompilerParams(
            collective_id=0, has_side_effects=True, vmem_limit_bytes=62 * 2**20
        ),
        name="memory_layer",
    )(
        retrieved.T, block_slot, gate_bias, queries, keys, values,
        mem_keys.reshape(blocked), mem_values.reshape(blocked), weight,
    )


def solution(mesh):
    in_specs = (
        P("dp", "tensor"),
        P("dp", "tensor"),
        P("dp", "tensor"),
        P("dp", "tensor"),
        P("dp", "tensor"),
        P("tensor"),
        P("tensor", None),
        P("dp", None),
        P(),
    )
    out_specs = P("tensor", "dp")
    return jax.shard_map(shards, mesh=mesh, in_specs=in_specs, out_specs=out_specs, check_vma=False)
```

```python
import functools
import math

import jax
import jax.numpy as jnp
from jax import lax
from jax.experimental import pallas as pl
from jax.experimental.pallas import tpu as pltpu
from jax.sharding import PartitionSpec as P

BLOCK = 128
SEG = 512
TOPK = 4
UNIQ_CAP = 4
CHUNK = 256
NEG = -3.0e38
MESH = pl.DeviceIdType.MESH
NT = (((1,), (1,)), ((), ()))
RANK_ROW = UNIQ_CAP
SLOT_ROW = UNIQ_CAP + 1


def flipped(index, mask):
    bit = 1
    result = index
    while bit <= mask:
        if mask & bit:
            result = result + bit * (1 - 2 * (lax.rem(lax.div(index, bit), 2)))
        bit *= 2
    return result


def at_least(value, bound):
    return lax.div(value - bound + 64, 64)


def layer_kernel(
    n, groups, heads, rung_minor, sliced,
    ret_ref, slot_ref, gate_ref, q_hbm, k_hbm, v_hbm, mk_hbm, mv_hbm, w_hbm,
    out_hbm,
    qb, kl, vl, vt, kown, vraw, vown, sk, sv, land_k, land_v, loc, po, st,
    o_out, s_out, o_in, s_in, wg, wt, acc, ag, out_vm, tab_in, tab_sm,
    in_sem, smem_sem, own_w_sem, out_sem, t_ss, t_rs, q_ss, q_rs, k_ss, k_rs, v_ss, v_rs,
    o_ss, o_rs, s_ss, s_rs, w_ss, w_rs, a_ss, a_rs, f_ss, f_rs,
):
    me = lax.axis_index("dp")
    tme = lax.axis_index("tensor")
    peers = 2 * n
    local_blocks = kown.shape[1]
    chunks, head = ag.shape[1], kl.shape[2]
    tok = kl.shape[1]
    feats = wg.shape[1]
    scale = head ** -0.5 * math.log2(math.e)

    def split(index):
        if rung_minor:
            return lax.div(index, 2), lax.rem(index, 2)
        return lax.rem(index, n), lax.div(index, n)

    def join(line, rung):
        return line * 2 + rung if rung_minor else rung * n + line

    z, x = split(me)
    mirror = join(z, 1 - x)
    half = lax.div(2 * z, n)
    near = z * (1 - half) + (n - 1 - z) * half

    def stage_flow(h, j):
        both = at_least(2 * near, j + 1)
        tau = both * (j // 2) + (1 - both) * (j - near)
        primary = both * (1 - j % 2) + (1 - both)
        right = primary * (1 - half) + (1 - primary) * half
        if h < heads - 1:
            return right, z + (tau + 1) * (2 * right - 1)
        return right, right * (n - 1 - tau) + (1 - right) * tau

    loads = []

    def load(src, dst):
        copy = pltpu.make_async_copy(src, dst, in_sem.at[len(loads)])
        copy.start()
        loads.append(copy)

    def cols(h):
        return pl.ds(h * head, head)

    for h in range(heads):
        load(q_hbm.at[:, cols(h)], qb.at[z, h])
    for h in range(heads):
        load(mk_hbm.at[:, :, cols(h)], kown.at[h])
    load(mv_hbm, vraw)
    for h in range(heads):
        load(k_hbm.at[:, cols(h)], kl.at[h])
    load(v_hbm, vl)

    barrier = pltpu.get_barrier_semaphore()
    for m in range(1, peers):
        pl.semaphore_signal(barrier, inc=1, device_id={"dp": flipped(me, m)}, device_id_type=MESH)
    for m in range(1, groups):
        pl.semaphore_signal(
            barrier, inc=1, device_id={"tensor": flipped(tme, m)}, device_id_type=MESH
        )

    wide = tab_in.shape[2]
    lane = lax.broadcasted_iota(jnp.int32, (8, wide), 1)
    sub = lax.broadcasted_iota(jnp.int32, (8, wide), 0)
    inner = lax.rem(lane, local_blocks)
    slots = jnp.zeros((8, wide), jnp.int32)
    present = jnp.zeros((8, wide), jnp.int32)
    for b in range(tok // BLOCK):
        for i in range(TOPK):
            slot = slot_ref[ret_ref[i, b]]
            slots = jnp.where(lane == b * TOPK + i, slot, slots)
            present = jnp.where(lane == slot, 1, present)
    rank = present
    shift = 1
    while shift < local_blocks:
        rank = rank + jnp.where(inner >= shift, pltpu.roll(rank, shift, 1), 0)
        shift *= 2
    rank = rank - present
    wanted = jnp.where((present == 1) & (rank == sub), inner, 0)
    shift = local_blocks // 2
    while shift >= 1:
        wanted = jnp.maximum(wanted, pltpu.roll(wanted, wide - shift, 1))
        shift //= 2
    table = jnp.where(sub < UNIQ_CAP, wanted, jnp.where(sub == RANK_ROW, rank, slots))
    tab_in[me] = table

    pl.semaphore_wait(barrier, peers - 1 + groups - 1)

    tables = []
    for m in range(1, peers):
        copy = pltpu.make_async_remote_copy(
            src_ref=tab_in.at[me], dst_ref=tab_in.at[me], send_sem=t_ss,
            recv_sem=t_rs.at[m], device_id={"dp": flipped(me, m)}, device_id_type=MESH,
        )
        copy.start()
        tables.append(copy)

    def tokens(c):
        return pl.ds(pl.multiple_of(c * CHUNK, CHUNK), CHUNK)

    def q_copy(right, source, h, c):
        part = qb.at[source, h, tokens(c)]
        return pltpu.make_async_remote_copy(
            src_ref=part, dst_ref=part, send_sem=q_ss.at[right, source],
            recv_sem=q_rs.at[source, h, c],
            device_id={"dp": join(z + 2 * right - 1, x)}, device_id_type=MESH,
        )

    def behind(right):
        return right * z + (1 - right) * (n - 1 - z)

    def ahead(right):
        return n - 1 - behind(right)

    def q_own(h, right, when):
        @pl.when(jnp.logical_and(ahead(right) > 0, when))
        def _():
            for c in range(chunks):
                q_copy(right, z, h, c).start()

    def q_pass(h, right, source, valid, c):
        @pl.when(jnp.logical_and(ahead(right) > 0, valid))
        def _():
            q_copy(right, source, h, c).wait_recv()
            q_copy(right, source, h, c).start()

    def q_near(k, c):
        for right in (1 - half, half):
            q_pass(0, right, z - k * (2 * right - 1), behind(right) >= k, c)

    def q_far(h, right, tau):
        source = right * tau + (1 - right) * (n - 1 - tau)

        def step(c, carry):
            q_pass(h, right, source, behind(right) > tau, c)
            return carry

        lax.fori_loop(0, chunks, step, 0)
        q_own(h, right, behind(right) == tau + 1)

    def loop(fn):
        def step(c, carry):
            fn(c)
            return carry

        lax.fori_loop(0, chunks, step, 0)

    def q_end(h, d):
        @pl.when(near == 0)
        def _():
            loop(lambda c: q_copy(half, d, h, c).wait_recv())

    for h in range(heads):
        loads[h].wait()
    for h in range(min(heads, 2)):
        for right in (1 - half, half):
            q_own(h, right, behind(right) == 0 if h else True)

    def weight_part(t):
        if sliced:
            return w_hbm.at[:, pl.ds(pl.multiple_of(t * feats, 128), feats)]
        return w_hbm.at[t]

    def group_rows(t):
        return pl.ds(pl.multiple_of(t * heads * head, 128), heads * head)

    w_copies = []
    for m in range(1, groups):
        peer = flipped(tme, m)
        copy = pltpu.make_async_remote_copy(
            src_ref=weight_part(peer), dst_ref=wg.at[group_rows(tme)],
            send_sem=w_ss.at[m], recv_sem=w_rs.at[m], device_id={"tensor": peer},
            device_id_type=MESH,
        )
        copy.start()
        w_copies.append(copy)
    own_w = pltpu.make_async_copy(weight_part(tme), wg.at[group_rows(tme)], own_w_sem)
    own_w.start()

    for h in range(heads):
        loads[heads + h].wait()
    loads[2 * heads].wait()

    def turn_values(i, carry):
        for h in range(heads):
            vown[h, i] = vraw[i, :, h * head:(h + 1) * head].T
        return carry

    lax.fori_loop(0, local_blocks, turn_values, 0)

    for copy in tables:
        copy.wait_recv()
    to_smem = pltpu.make_async_copy(tab_in, tab_sm, smem_sem)
    to_smem.start()
    to_smem.wait()

    ships = {}
    for h in range(heads):
        for j in range(n):
            d = z if j == n - 1 else stage_flow(h, j)[1]
            reader = join(d, 1 - x)
            for key, own, send, land, ss, rs in (
                ("k", kown, sk, land_k, k_ss, k_rs), ("v", vown, sv, land_v, v_ss, v_rs)
            ):
                for c in range(UNIQ_CAP):
                    send[h, j, c] = own[h, tab_sm[reader, c, me * local_blocks]]
                copy = pltpu.make_async_remote_copy(
                    src_ref=send.at[h, j], dst_ref=land[h][j].at[pl.ds(UNIQ_CAP, UNIQ_CAP)],
                    send_sem=ss, recv_sem=rs.at[h, j], device_id={"dp": mirror},
                    device_id_type=MESH,
                )
                copy.start()
                ships[key, h, j] = copy

    for copy in loads[2 * heads + 1:]:
        copy.wait()

    def turn_local(i, carry):
        rows = pl.ds(pl.multiple_of(i * BLOCK, BLOCK), BLOCK)
        for h in range(heads):
            vt[h, i] = vl[rows, h * head:(h + 1) * head].T
        return carry

    lax.fori_loop(0, tok // BLOCK, turn_local, 0)

    def gate(h, width):
        bias = jnp.full((1, width), gate_ref[h], jnp.float32)
        return 1.0 / (1.0 + jnp.exp(-bias))

    blocks_seg = SEG // BLOCK
    per_chunk = CHUNK // BLOCK

    def local_segment(u, carry):
        s, h = lax.div(u, heads), lax.rem(u, heads)
        first = s * blocks_seg
        key_row = lax.broadcasted_iota(jnp.int32, (BLOCK, BLOCK), 0)
        query_col = lax.broadcasted_iota(jnp.int32, (BLOCK, BLOCK), 1)
        keep = 1.0 - gate(h, BLOCK)
        for i in range(blocks_seg):
            span = (i + 1) * BLOCK
            base = pl.multiple_of(s * SEG, SEG)
            scores = lax.dot_general(
                kl[h, pl.ds(base, span)], qb[z, h, pl.ds(base + i * BLOCK, BLOCK)], NT,
                preferred_element_type=jnp.float32,
            )
            last = jnp.where(key_row <= query_col, scores[i * BLOCK:], -jnp.inf)
            scores = last if i == 0 else jnp.concatenate([scores[:i * BLOCK], last], axis=0)
            top = jnp.max(scores, axis=0, keepdims=True)
            weights = jnp.exp2((scores - top) * scale)
            total = jnp.sum(weights, axis=0, keepdims=True)
            vals = jnp.concatenate([vt[h, first + g] for g in range(i + 1)], axis=1)
            out = jnp.dot(
                vals, weights.astype(jnp.bfloat16), preferred_element_type=jnp.float32
            )
            loc[h, first + i] = out * (keep / total)
        q_near(1, u)
        return carry

    lax.fori_loop(0, chunks, local_segment, 0)
    for k in range(2, n - 1):
        loop(functools.partial(q_near, k))
    if heads > 1:
        q_far(1, 1 - half, 0)

    def partial_block(h, j, d, b):
        owner_at = join(d, x)
        places, valid = [], []
        for i in range(TOPK):
            slot = tab_sm[owner_at, SLOT_ROW, b * TOPK + i]
            line, rung = split(lax.div(slot, local_blocks))
            side = lax.rem(rung + x, 2)
            places.append(side * UNIQ_CAP + tab_sm[owner_at, RANK_ROW, slot])
            valid.append(line == z)
        keys = jnp.concatenate([land_k[h][j][p] for p in places], axis=0)
        rows = pl.ds(pl.multiple_of(b * BLOCK, BLOCK), BLOCK)
        scores = lax.dot_general(keys, qb[d, h, rows], NT, preferred_element_type=jnp.float32)
        scores = jnp.concatenate(
            [
                jnp.where(valid[i], scores[i * BLOCK:(i + 1) * BLOCK], NEG)
                for i in range(TOPK)
            ],
            axis=0,
        )
        top = jnp.max(scores, axis=0, keepdims=True)
        weights = jnp.exp2((scores - top) * scale)
        total = jnp.sum(weights, axis=0, keepdims=True)
        vals = jnp.concatenate([land_v[h][j][p] for p in places], axis=1)
        out = jnp.dot(vals, weights.astype(jnp.bfloat16), preferred_element_type=jnp.float32)
        return out, top, total

    def lanes(blk):
        return slice(blk * BLOCK, (blk + 1) * BLOCK)

    def partial_chunk(h, j, d, c):
        tops, totals = [], []
        for blk in range(per_chunk):
            out, top, total = partial_block(h, j, d, c * per_chunk + blk)
            po[d, c, :, lanes(blk)] = out
            tops.append(top)
            totals.append(total)
        st[d, c] = jnp.concatenate(tops + totals, axis=0)

    def merged(right, d, h, c):
        o_copy(right, d, h, c).wait_recv()
        s_copy(right, d, h, c).wait_recv()
        stats, stats_in = st[d, c], s_in[right, d, h, c]
        top, total = stats[:per_chunk], stats[per_chunk:]
        top_in, total_in = stats_in[:per_chunk], stats_in[per_chunk:]
        new = jnp.maximum(top, top_in)
        mine = jnp.exp2((top - new) * scale)
        theirs = jnp.exp2((top_in - new) * scale)
        parts = [
            po[d, c, :, lanes(blk)] * mine[blk:blk + 1]
            + o_in[right, d, h, c, :, lanes(blk)].astype(jnp.float32) * theirs[blk:blk + 1]
            for blk in range(per_chunk)
        ]
        stats = jnp.concatenate([new, total * mine + total_in * theirs], axis=0)
        return jnp.concatenate(parts, axis=1), stats

    def o_copy(right, d, h, c):
        return pltpu.make_async_remote_copy(
            src_ref=o_out.at[h, d, c], dst_ref=o_in.at[right, d, h, c],
            send_sem=o_ss, recv_sem=o_rs.at[right, d, h, c],
            device_id={"dp": join(z + 2 * right - 1, x)}, device_id_type=MESH,
        )

    def s_copy(right, d, h, c):
        return pltpu.make_async_remote_copy(
            src_ref=s_out.at[h, d, c], dst_ref=s_in.at[right, d, h, c],
            send_sem=s_ss, recv_sem=s_rs.at[right, d, h, c],
            device_id={"dp": join(z + 2 * right - 1, x)}, device_id_type=MESH,
        )

    def group_head(t):
        return pl.ds(pl.multiple_of(t * head, 128), head)

    def a_copy(h, c, m):
        part = ag.at[h, c, group_head(tme)]
        return pltpu.make_async_remote_copy(
            src_ref=part, dst_ref=part, send_sem=a_ss.at[m // 2], recv_sem=a_rs.at[h, c, m // 2],
            device_id={"tensor": flipped(tme, m)}, device_id_type=MESH,
        )

    def f_copy(h, c, m):
        part = ag.at[h, c, group_head(flipped(tme, m))]
        return pltpu.make_async_remote_copy(
            src_ref=part, dst_ref=part, send_sem=f_ss.at[m // 2], recv_sem=f_rs.at[h, c, m // 2],
            device_id={"tensor": flipped(tme, 1)}, device_id_type=MESH,
        )

    others = list(range(2, groups, 2))

    def arrive(h, j, d):
        ships["k", h, j].wait_recv()
        ships["v", h, j].wait_recv()
        reader = join(d, x)
        for c in range(UNIQ_CAP):
            at = tab_sm[reader, c, me * local_blocks]
            land_k[h][j][c] = kown[h, at]
            land_v[h][j][c] = vown[h, at]

    def pass_on(h, right, d, c):
        starts = behind(right) == 0

        @pl.when(starts)
        def _():
            o_out[h, d, c] = po[d, c].astype(o_out.dtype)
            s_out[h, d, c] = st[d, c]

        @pl.when(jnp.logical_not(starts))
        def _():
            out, stats = merged(right, d, h, c)
            o_out[h, d, c] = out.astype(o_out.dtype)
            s_out[h, d, c] = stats

        o_copy(right, d, h, c).start()
        s_copy(right, d, h, c).start()

    def last_stage(h, j):
        right, d = stage_flow(h, j)
        arrive(h, j, d)
        q_end(h, d)

        def chunk(c, carry):
            partial_chunk(h, j, d, c)
            pass_on(h, right, d, c)
            return carry

        lax.fori_loop(0, chunks, chunk, 0)

    def due(j, right):
        d = right * (j + 1) + (1 - right) * (n - 2 - j)
        return d, right * (d - z) + (1 - right) * (z - d) > 0

    def early_stage(h, j):
        d = stage_flow(h, j)[1]
        arrive(h, j, d)
        q_end(h, d)
        first, passes = due(j, 1 - half)

        def chunk(c, carry):
            partial_chunk(h, j, d, c)

            @pl.when(passes)
            def _():
                pass_on(h, 1 - half, first, c)

            return carry

        lax.fori_loop(0, chunks, chunk, 0)

    def early_rest(h, j):
        second, passes = due(j, half)

        @pl.when(passes)
        def _():
            def chunk(c, carry):
                pass_on(h, half, second, c)
                return carry

            lax.fori_loop(0, chunks, chunk, 0)

    def own_partial(h):
        arrive(h, n - 1, z)
        loop(lambda c: partial_chunk(h, n - 1, z, c))

    def own_final(h):
        loop(functools.partial(finish_chunk, h))

    def own_stage(h):
        arrive(h, n - 1, z)

        def chunk(c):
            partial_chunk(h, n - 1, z, c)
            finish_chunk(h, c)

        loop(chunk)

    def finish_chunk(h, c):
        for right in (1 - half, half):
            @pl.when(behind(right) > 0)
            def _():
                po[z, c], st[z, c] = merged(right, z, h, c)

        for blk in range(per_chunk):
            weight = gate(h, BLOCK) / st[z, c, per_chunk + blk:per_chunk + blk + 1]
            result = po[z, c, :, lanes(blk)] * weight + loc[h, c * per_chunk + blk]
            ag[h, c, group_head(tme), lanes(blk)] = result.astype(ag.dtype)
        for m in others + [1]:
            a_copy(h, c, m).start()

    def forward(h, c):
        for m in others:
            a_copy_from(h, c, m).wait_recv()
            f_copy(h, c, m).start()

    def a_copy_from(h, c, m):
        part = ag.at[h, c, group_head(flipped(tme, m))]
        return pltpu.make_async_remote_copy(
            src_ref=part, dst_ref=part, send_sem=a_ss.at[m // 2], recv_sem=a_rs.at[h, c, m // 2],
            device_id={"tensor": flipped(tme, m)}, device_id_type=MESH,
        )

    def f_copy_from(h, c, m):
        part = ag.at[h, c, group_head(flipped(flipped(tme, 1), m))]
        return pltpu.make_async_remote_copy(
            src_ref=part, dst_ref=part, send_sem=f_ss.at[m // 2], recv_sem=f_rs.at[h, c, m // 2],
            device_id={"tensor": flipped(tme, 1)}, device_id_type=MESH,
        )

    turn = 128 if feats % 128 == 0 else feats

    def out_copy(c):
        return pltpu.make_async_copy(out_vm.at[c], out_hbm.at[:, tokens(c)], out_sem.at[c])

    def settle(h, c):
        a_copy_from(h, c, 1).wait_recv()
        for m in others:
            f_copy_from(h, c, m).wait_recv()

    def project(parts, c):
        out = acc[c] if heads - 1 in parts and heads > 1 else None
        for h in parts:
            term = jnp.dot(wt[h], ag[h, c], preferred_element_type=jnp.float32)
            out = term if out is None else out + term
        if heads - 1 in parts:
            out_vm[c] = out.astype(out_vm.dtype)
        else:
            acc[c] = out

    def turn_weights(i, carry):
        at = pl.ds(pl.multiple_of(i * turn, turn), turn) if turn < feats else slice(None)
        for t in range(groups):
            for h in range(heads):
                rows = slice((t * heads + h) * head, (t * heads + h + 1) * head)
                wt[h, at, t * head:(t + 1) * head] = wg[rows, at].T
        return carry

    for h in range(heads - 1):
        for j in range(n - 1):
            early_stage(h, j)
            if j < n - 2:
                q_far(h + 1, half, j)
                if j < n - 3:
                    q_far(h + 1, 1 - half, j + 1)
            early_rest(h, j)
        own_partial(h)

    h = heads - 1
    for j in range(n - 1):
        last_stage(h, j)
        if j == n - 3:
            for early in range(heads - 1):
                own_final(early)
            for copy in w_copies:
                copy.wait()
            own_w.wait()
            lax.fori_loop(0, feats // turn, turn_weights, 0)
    for early in range(heads - 1):
        loop(functools.partial(forward, early))

    def project_early(c):
        for early in range(heads - 1):
            settle(early, c)
        project(range(heads - 1), c)

    loop(project_early)
    own_stage(h)
    forward(h, 0)

    def finish(c):
        @pl.when(c < chunks - 1)
        def _():
            forward(h, c + 1)

        settle(h, c)
        project([h], c)
        out_copy(c).start()

    loop(finish)

    def drain(part, sem):
        pltpu.make_async_copy(part, part, sem).wait()

    drain(tab_in.at[pl.ds(0, peers - 1)], t_ss)
    drain(sk, k_ss)
    drain(sv, v_ss)

    for right in (1, 0):
        for k in range(n):
            source = z - k * (2 * right - 1)

            @pl.when(jnp.logical_and(behind(right) >= k, ahead(right) > 0))
            def _():
                drain(qb.at[source], q_ss.at[right, source])

    drain(o_out.at[:, pl.ds(0, n - 1)], o_ss)
    drain(s_out.at[:, pl.ds(0, n - 1)], s_ss)
    for m in others + [1]:
        drain(ag.at[:, :, group_head(tme)], a_ss.at[m // 2])
    for m in others:
        drain(ag.at[:, :, group_head(tme)], f_ss.at[m // 2])
    for c in range(chunks):
        out_copy(c).wait()


def shards(
    queries, keys, values, mem_keys, mem_values, gate_bias, out_weight, retrieved, block_slot
):
    tok, width = queries.shape
    heads = gate_bias.shape[0]
    head = width // heads
    peers = lax.axis_size("dp")
    groups = lax.axis_size("tensor")
    n = peers // 2
    local_blocks = mem_keys.shape[0] // BLOCK
    feats = out_weight.shape[1] // groups
    chunks = tok // CHUNK
    sliced = feats % 128 == 0
    weight = out_weight
    if not sliced:
        weight = out_weight.reshape(width, groups, feats).transpose(1, 0, 2)
    blocked = (local_blocks, BLOCK, width)
    bf16, f32 = jnp.bfloat16, jnp.float32
    landing = pltpu.VMEM((2 * UNIQ_CAP, BLOCK, head), bf16)
    landings = tuple(tuple(landing for _ in range(n)) for _ in range(heads))
    wide = block_slot.shape[0]
    stat_rows = 2 * CHUNK // BLOCK
    dma = pltpu.SemaphoreType.DMA
    smem = pl.BlockSpec(memory_space=pltpu.SMEM)
    any_spec = pl.BlockSpec(memory_space=pltpu.HBM)
    return pl.pallas_call(
        functools.partial(layer_kernel, n, groups, heads, peers <= 8, sliced),
        out_shape=jax.ShapeDtypeStruct((feats, tok), bf16),
        in_specs=[smem] * 3 + [any_spec] * 6,
        out_specs=any_spec,
        scratch_shapes=[
            pltpu.VMEM((n, heads, tok, head), bf16),
            pltpu.VMEM((heads, tok, head), bf16),
            pltpu.VMEM((tok, width), bf16),
            pltpu.VMEM((heads, tok // BLOCK, head, BLOCK), bf16),
            pltpu.VMEM((heads, local_blocks, BLOCK, head), bf16),
            pltpu.VMEM(blocked, bf16),
            pltpu.VMEM((heads, local_blocks, head, BLOCK), bf16),
            pltpu.VMEM((heads, n, UNIQ_CAP, BLOCK, head), bf16),
            pltpu.VMEM((heads, n, UNIQ_CAP, head, BLOCK), bf16),
            landings,
            landings,
            pltpu.VMEM((heads, tok // BLOCK, head, BLOCK), f32),
            pltpu.VMEM((n, chunks, head, CHUNK), f32),
            pltpu.VMEM((n, chunks, stat_rows, BLOCK), f32),
            pltpu.VMEM((heads, n, chunks, head, CHUNK), bf16),
            pltpu.VMEM((heads, n, chunks, stat_rows, BLOCK), f32),
            pltpu.VMEM((2, n, heads, chunks, head, CHUNK), bf16),
            pltpu.VMEM((2, n, heads, chunks, stat_rows, BLOCK), f32),
            pltpu.VMEM((groups * width, feats), bf16),
            pltpu.VMEM((heads, feats, groups * head), bf16),
            pltpu.VMEM((chunks, feats, CHUNK), f32),
            pltpu.VMEM((heads, chunks, groups * head, CHUNK), bf16),
            pltpu.VMEM((chunks, feats, CHUNK), bf16),
            pltpu.VMEM((peers, 8, wide), jnp.int32),
            pltpu.SMEM((peers, 8, wide), jnp.int32),
            dma((3 * heads + 2,)),
            dma(()),
            dma(()),
            dma((chunks,)),
            dma(()),
            dma((peers,)),
            dma((2, n)),
            dma((n, heads, chunks)),
            dma(()),
            dma((heads, n)),
            dma(()),
            dma((heads, n)),
            dma(()),
            dma((2, n, heads, chunks)),
            dma(()),
            dma((2, n, heads, chunks)),
            dma((groups,)),
            dma((groups,)),
            dma((groups // 2,)),
            dma((heads, chunks, groups // 2)),
            dma((groups // 2,)),
            dma((heads, chunks, groups // 2)),
        ],
        compiler_params=pltpu.CompilerParams(
            collective_id=0, has_side_effects=True, vmem_limit_bytes=62 * 2**20
        ),
        name="memory_layer",
    )(
        retrieved.T, block_slot, gate_bias, queries, keys, values,
        mem_keys.reshape(blocked), mem_values.reshape(blocked), weight,
    )


def solution(mesh):
    in_specs = (
        P("dp", "tensor"),
        P("dp", "tensor"),
        P("dp", "tensor"),
        P("dp", "tensor"),
        P("dp", "tensor"),
        P("tensor"),
        P("tensor", None),
        P("dp", None),
        P(),
    )
    out_specs = P("tensor", "dp")
    return jax.shard_map(shards, mesh=mesh, in_specs=in_specs, out_specs=out_specs, check_vma=False)
```

```python
import functools
import math

import jax
import jax.numpy as jnp
from jax import lax
from jax.experimental import pallas as pl
from jax.experimental.pallas import tpu as pltpu
from jax.sharding import PartitionSpec as P

BLOCK = 128
SEG = 512
TOPK = 4
UNIQ_CAP = 4
CHUNK = 256
NEG = -3.0e38
MESH = pl.DeviceIdType.MESH
NT = (((1,), (1,)), ((), ()))
RANK_ROW = UNIQ_CAP
SLOT_ROW = UNIQ_CAP + 1


def flipped(index, mask):
    bit = 1
    result = index
    while bit <= mask:
        if mask & bit:
            result = result + bit * (1 - 2 * (lax.rem(lax.div(index, bit), 2)))
        bit *= 2
    return result


def at_least(value, bound):
    return lax.div(value - bound + 64, 64)


def layer_kernel(
    n, groups, heads, rung_minor, sliced,
    ret_ref, slot_ref, gate_ref, q_hbm, k_hbm, v_hbm, mk_hbm, mv_hbm, w_hbm,
    out_hbm,
    qb, kl, vl, vt, kown, vraw, vown, sk, sv, land_k, land_v, loc, po, st,
    o_out, s_out, o_in, s_in, wg, wt, acc, ag, out_vm, tab_in, tab_sm,
    in_sem, smem_sem, own_w_sem, out_sem, t_ss, t_rs, q_ss, q_rs, k_ss, k_rs, v_ss, v_rs,
    o_ss, o_rs, s_ss, s_rs, w_ss, w_rs, a_ss, a_rs, f_ss, f_rs,
):
    me = lax.axis_index("dp")
    tme = lax.axis_index("tensor")
    peers = 2 * n
    local_blocks = kown.shape[1]
    chunks, head = ag.shape[1], kl.shape[2]
    tok = kl.shape[1]
    feats = wg.shape[1]
    scale = head ** -0.5 * math.log2(math.e)

    def split(index):
        if rung_minor:
            return lax.div(index, 2), lax.rem(index, 2)
        return lax.rem(index, n), lax.div(index, n)

    def join(line, rung):
        return line * 2 + rung if rung_minor else rung * n + line

    z, x = split(me)
    mirror = join(z, 1 - x)
    half = lax.div(2 * z, n)
    near = z * (1 - half) + (n - 1 - z) * half

    def stage_flow(h, j):
        both = at_least(2 * near, j + 1)
        tau = both * (j // 2) + (1 - both) * (j - near)
        primary = both * (1 - j % 2) + (1 - both)
        right = primary * (1 - half) + (1 - primary) * half
        if h < heads - 1:
            return right, z + (tau + 1) * (2 * right - 1)
        return right, right * (n - 1 - tau) + (1 - right) * tau

    loads = []

    def load(src, dst):
        copy = pltpu.make_async_copy(src, dst, in_sem.at[len(loads)])
        copy.start()
        loads.append(copy)

    def cols(h):
        return pl.ds(h * head, head)

    for h in range(heads):
        load(q_hbm.at[:, cols(h)], qb.at[z, h])
    for h in range(heads):
        load(mk_hbm.at[:, :, cols(h)], kown.at[h])
    load(mv_hbm, vraw)
    for h in range(heads):
        load(k_hbm.at[:, cols(h)], kl.at[h])
    load(v_hbm, vl)

    barrier = pltpu.get_barrier_semaphore()
    for m in range(1, peers):
        pl.semaphore_signal(barrier, inc=1, device_id={"dp": flipped(me, m)}, device_id_type=MESH)
    for m in range(1, groups):
        pl.semaphore_signal(
            barrier, inc=1, device_id={"tensor": flipped(tme, m)}, device_id_type=MESH
        )

    wide = tab_in.shape[2]
    lane = lax.broadcasted_iota(jnp.int32, (8, wide), 1)
    sub = lax.broadcasted_iota(jnp.int32, (8, wide), 0)
    inner = lax.rem(lane, local_blocks)
    slots = jnp.zeros((8, wide), jnp.int32)
    present = jnp.zeros((8, wide), jnp.int32)
    for b in range(tok // BLOCK):
        for i in range(TOPK):
            slot = slot_ref[ret_ref[i, b]]
            slots = jnp.where(lane == b * TOPK + i, slot, slots)
            present = jnp.where(lane == slot, 1, present)
    rank = present
    shift = 1
    while shift < local_blocks:
        rank = rank + jnp.where(inner >= shift, pltpu.roll(rank, shift, 1), 0)
        shift *= 2
    rank = rank - present
    wanted = jnp.where((present == 1) & (rank == sub), inner, 0)
    shift = local_blocks // 2
    while shift >= 1:
        wanted = jnp.maximum(wanted, pltpu.roll(wanted, wide - shift, 1))
        shift //= 2
    table = jnp.where(sub < UNIQ_CAP, wanted, jnp.where(sub == RANK_ROW, rank, slots))
    tab_in[me] = table

    pl.semaphore_wait(barrier, peers - 1 + groups - 1)

    tables = []
    for m in range(1, peers):
        copy = pltpu.make_async_remote_copy(
            src_ref=tab_in.at[me], dst_ref=tab_in.at[me], send_sem=t_ss,
            recv_sem=t_rs.at[m], device_id={"dp": flipped(me, m)}, device_id_type=MESH,
        )
        copy.start()
        tables.append(copy)

    def tokens(c):
        return pl.ds(pl.multiple_of(c * CHUNK, CHUNK), CHUNK)

    def q_copy(right, source, h, c):
        part = qb.at[source, h, tokens(c)]
        return pltpu.make_async_remote_copy(
            src_ref=part, dst_ref=part, send_sem=q_ss.at[right, source],
            recv_sem=q_rs.at[source, h, c],
            device_id={"dp": join(z + 2 * right - 1, x)}, device_id_type=MESH,
        )

    def behind(right):
        return right * z + (1 - right) * (n - 1 - z)

    def ahead(right):
        return n - 1 - behind(right)

    def q_own(h, right, when):
        @pl.when(jnp.logical_and(ahead(right) > 0, when))
        def _():
            for c in range(chunks):
                q_copy(right, z, h, c).start()

    def q_pass(h, right, source, valid, c):
        @pl.when(jnp.logical_and(ahead(right) > 0, valid))
        def _():
            q_copy(right, source, h, c).wait_recv()
            q_copy(right, source, h, c).start()

    def q_near(k, c):
        for right in (1 - half, half):
            q_pass(0, right, z - k * (2 * right - 1), behind(right) >= k, c)

    def q_far(h, right, tau):
        source = right * tau + (1 - right) * (n - 1 - tau)

        def step(c, carry):
            q_pass(h, right, source, behind(right) > tau, c)
            return carry

        lax.fori_loop(0, chunks, step, 0)
        q_own(h, right, behind(right) == tau + 1)

    def loop(fn):
        def step(c, carry):
            fn(c)
            return carry

        lax.fori_loop(0, chunks, step, 0)

    def q_end(h, d):
        @pl.when(near == 0)
        def _():
            loop(lambda c: q_copy(half, d, h, c).wait_recv())

    for h in range(heads):
        loads[h].wait()
    for h in range(min(heads, 2)):
        for right in (1 - half, half):
            q_own(h, right, behind(right) == 0 if h else True)

    def weight_part(t):
        if sliced:
            return w_hbm.at[:, pl.ds(pl.multiple_of(t * feats, 128), feats)]
        return w_hbm.at[t]

    def group_rows(t):
        return pl.ds(pl.multiple_of(t * heads * head, 128), heads * head)

    w_copies = []
    for m in range(1, groups):
        peer = flipped(tme, m)
        copy = pltpu.make_async_remote_copy(
            src_ref=weight_part(peer), dst_ref=wg.at[group_rows(tme)],
            send_sem=w_ss.at[m], recv_sem=w_rs.at[m], device_id={"tensor": peer},
            device_id_type=MESH,
        )
        copy.start()
        w_copies.append(copy)
    own_w = pltpu.make_async_copy(weight_part(tme), wg.at[group_rows(tme)], own_w_sem)
    own_w.start()

    for h in range(heads):
        loads[heads + h].wait()
    loads[2 * heads].wait()

    def turn_values(i, carry):
        for h in range(heads):
            vown[h, i] = vraw[i, :, h * head:(h + 1) * head].T
        return carry

    lax.fori_loop(0, local_blocks, turn_values, 0)

    for copy in tables:
        copy.wait_recv()
    to_smem = pltpu.make_async_copy(tab_in, tab_sm, smem_sem)
    to_smem.start()
    to_smem.wait()

    ships = {}
    for h in range(heads):
        for j in range(n):
            d = z if j == n - 1 else stage_flow(h, j)[1]
            reader = join(d, 1 - x)
            for key, own, send, land, ss, rs in (
                ("k", kown, sk, land_k, k_ss, k_rs), ("v", vown, sv, land_v, v_ss, v_rs)
            ):
                for c in range(UNIQ_CAP):
                    send[h, j, c] = own[h, tab_sm[reader, c, me * local_blocks]]
                copy = pltpu.make_async_remote_copy(
                    src_ref=send.at[h, j], dst_ref=land[h][j].at[pl.ds(UNIQ_CAP, UNIQ_CAP)],
                    send_sem=ss, recv_sem=rs.at[h, j], device_id={"dp": mirror},
                    device_id_type=MESH,
                )
                copy.start()
                ships[key, h, j] = copy

    for copy in loads[2 * heads + 1:]:
        copy.wait()

    def turn_local(i, carry):
        rows = pl.ds(pl.multiple_of(i * BLOCK, BLOCK), BLOCK)
        for h in range(heads):
            vt[h, i] = vl[rows, h * head:(h + 1) * head].T
        return carry

    lax.fori_loop(0, tok // BLOCK, turn_local, 0)

    def gate(h, width):
        bias = jnp.full((1, width), gate_ref[h], jnp.float32)
        return 1.0 / (1.0 + jnp.exp(-bias))

    blocks_seg = SEG // BLOCK
    per_chunk = CHUNK // BLOCK

    def local_segment(u, carry):
        s, h = lax.div(u, heads), lax.rem(u, heads)
        first = s * blocks_seg
        key_row = lax.broadcasted_iota(jnp.int32, (BLOCK, BLOCK), 0)
        query_col = lax.broadcasted_iota(jnp.int32, (BLOCK, BLOCK), 1)
        keep = 1.0 - gate(h, BLOCK)
        for i in range(blocks_seg):
            span = (i + 1) * BLOCK
            base = pl.multiple_of(s * SEG, SEG)
            scores = lax.dot_general(
                kl[h, pl.ds(base, span)], qb[z, h, pl.ds(base + i * BLOCK, BLOCK)], NT,
                preferred_element_type=jnp.float32,
            )
            last = jnp.where(key_row <= query_col, scores[i * BLOCK:], -jnp.inf)
            scores = last if i == 0 else jnp.concatenate([scores[:i * BLOCK], last], axis=0)
            top = jnp.max(scores, axis=0, keepdims=True)
            weights = jnp.exp2((scores - top) * scale)
            total = jnp.sum(weights, axis=0, keepdims=True)
            vals = jnp.concatenate([vt[h, first + g] for g in range(i + 1)], axis=1)
            out = jnp.dot(
                vals, weights.astype(jnp.bfloat16), preferred_element_type=jnp.float32
            )
            loc[h, first + i] = out * (keep / total)
        q_near(1, u)
        return carry

    lax.fori_loop(0, chunks, local_segment, 0)
    for k in range(2, n - 1):
        loop(functools.partial(q_near, k))
    if heads > 1:
        q_far(1, 1 - half, 0)

    def partial_block(h, j, d, b):
        owner_at = join(d, x)
        places, valid = [], []
        for i in range(TOPK):
            slot = tab_sm[owner_at, SLOT_ROW, b * TOPK + i]
            line, rung = split(lax.div(slot, local_blocks))
            side = lax.rem(rung + x, 2)
            places.append(side * UNIQ_CAP + tab_sm[owner_at, RANK_ROW, slot])
            valid.append(line == z)
        keys = jnp.concatenate([land_k[h][j][p] for p in places], axis=0)
        rows = pl.ds(pl.multiple_of(b * BLOCK, BLOCK), BLOCK)
        scores = lax.dot_general(keys, qb[d, h, rows], NT, preferred_element_type=jnp.float32)
        scores = jnp.concatenate(
            [
                jnp.where(valid[i], scores[i * BLOCK:(i + 1) * BLOCK], NEG)
                for i in range(TOPK)
            ],
            axis=0,
        )
        top = jnp.max(scores, axis=0, keepdims=True)
        weights = jnp.exp2((scores - top) * scale)
        total = jnp.sum(weights, axis=0, keepdims=True)
        vals = jnp.concatenate([land_v[h][j][p] for p in places], axis=1)
        out = jnp.dot(vals, weights.astype(jnp.bfloat16), preferred_element_type=jnp.float32)
        return out, top, total

    def lanes(blk):
        return slice(blk * BLOCK, (blk + 1) * BLOCK)

    def partial_chunk(h, j, d, c):
        tops, totals = [], []
        for blk in range(per_chunk):
            out, top, total = partial_block(h, j, d, c * per_chunk + blk)
            po[d, c, :, lanes(blk)] = out
            tops.append(top)
            totals.append(total)
        st[d, c] = jnp.concatenate(tops + totals, axis=0)

    def merged(right, d, h, c):
        o_copy(right, d, h, c).wait_recv()
        s_copy(right, d, h, c).wait_recv()
        stats, stats_in = st[d, c], s_in[right, d, h, c]
        top, total = stats[:per_chunk], stats[per_chunk:]
        top_in, total_in = stats_in[:per_chunk], stats_in[per_chunk:]
        new = jnp.maximum(top, top_in)
        mine = jnp.exp2((top - new) * scale)
        theirs = jnp.exp2((top_in - new) * scale)
        parts = [
            po[d, c, :, lanes(blk)] * mine[blk:blk + 1]
            + o_in[right, d, h, c, :, lanes(blk)].astype(jnp.float32) * theirs[blk:blk + 1]
            for blk in range(per_chunk)
        ]
        stats = jnp.concatenate([new, total * mine + total_in * theirs], axis=0)
        return jnp.concatenate(parts, axis=1), stats

    def o_copy(right, d, h, c):
        return pltpu.make_async_remote_copy(
            src_ref=o_out.at[h, d, c], dst_ref=o_in.at[right, d, h, c],
            send_sem=o_ss, recv_sem=o_rs.at[right, d, h, c],
            device_id={"dp": join(z + 2 * right - 1, x)}, device_id_type=MESH,
        )

    def s_copy(right, d, h, c):
        return pltpu.make_async_remote_copy(
            src_ref=s_out.at[h, d, c], dst_ref=s_in.at[right, d, h, c],
            send_sem=s_ss, recv_sem=s_rs.at[right, d, h, c],
            device_id={"dp": join(z + 2 * right - 1, x)}, device_id_type=MESH,
        )

    def group_head(t):
        return pl.ds(pl.multiple_of(t * head, 128), head)

    def a_copy(h, c, m):
        part = ag.at[h, c, group_head(tme)]
        return pltpu.make_async_remote_copy(
            src_ref=part, dst_ref=part, send_sem=a_ss.at[m // 2], recv_sem=a_rs.at[h, c, m // 2],
            device_id={"tensor": flipped(tme, m)}, device_id_type=MESH,
        )

    def f_copy(h, c, m):
        part = ag.at[h, c, group_head(flipped(tme, m))]
        return pltpu.make_async_remote_copy(
            src_ref=part, dst_ref=part, send_sem=f_ss.at[m // 2], recv_sem=f_rs.at[h, c, m // 2],
            device_id={"tensor": flipped(tme, 1)}, device_id_type=MESH,
        )

    others = list(range(2, groups, 2))

    def arrive(h, j, d):
        ships["k", h, j].wait_recv()
        ships["v", h, j].wait_recv()
        reader = join(d, x)
        for c in range(UNIQ_CAP):
            at = tab_sm[reader, c, me * local_blocks]
            land_k[h][j][c] = kown[h, at]
            land_v[h][j][c] = vown[h, at]

    def pass_on(h, right, d, c):
        starts = behind(right) == 0

        @pl.when(starts)
        def _():
            o_out[h, d, c] = po[d, c].astype(o_out.dtype)
            s_out[h, d, c] = st[d, c]

        @pl.when(jnp.logical_not(starts))
        def _():
            out, stats = merged(right, d, h, c)
            o_out[h, d, c] = out.astype(o_out.dtype)
            s_out[h, d, c] = stats

        o_copy(right, d, h, c).start()
        s_copy(right, d, h, c).start()

    def last_stage(h, j):
        right, d = stage_flow(h, j)
        arrive(h, j, d)
        q_end(h, d)

        def chunk(c, carry):
            partial_chunk(h, j, d, c)
            pass_on(h, right, d, c)
            return carry

        lax.fori_loop(0, chunks, chunk, 0)

    def due(j, right):
        d = right * (j + 1) + (1 - right) * (n - 2 - j)
        return d, right * (d - z) + (1 - right) * (z - d) > 0

    def early_stage(h, j):
        d = stage_flow(h, j)[1]
        arrive(h, j, d)
        q_end(h, d)
        first, passes = due(j, 1 - half)

        def chunk(c, carry):
            partial_chunk(h, j, d, c)

            @pl.when(passes)
            def _():
                pass_on(h, 1 - half, first, c)

            return carry

        lax.fori_loop(0, chunks, chunk, 0)

    def early_rest(h, j):
        second, passes = due(j, half)

        @pl.when(passes)
        def _():
            def chunk(c, carry):
                pass_on(h, half, second, c)
                return carry

            lax.fori_loop(0, chunks, chunk, 0)

    def own_partial(h):
        arrive(h, n - 1, z)
        loop(lambda c: partial_chunk(h, n - 1, z, c))

    def own_final(h):
        loop(functools.partial(finish_chunk, h))

    def own_stage(h):
        arrive(h, n - 1, z)

        def chunk(c):
            partial_chunk(h, n - 1, z, c)
            finish_chunk(h, c)

        loop(chunk)

    def finish_chunk(h, c):
        for right in (1 - half, half):
            @pl.when(behind(right) > 0)
            def _():
                po[z, c], st[z, c] = merged(right, z, h, c)

        for blk in range(per_chunk):
            weight = gate(h, BLOCK) / st[z, c, per_chunk + blk:per_chunk + blk + 1]
            result = po[z, c, :, lanes(blk)] * weight + loc[h, c * per_chunk + blk]
            ag[h, c, group_head(tme), lanes(blk)] = result.astype(ag.dtype)
        for m in others + [1]:
            a_copy(h, c, m).start()

    def forward(h, c):
        for m in others:
            a_copy_from(h, c, m).wait_recv()
            f_copy(h, c, m).start()

    def a_copy_from(h, c, m):
        part = ag.at[h, c, group_head(flipped(tme, m))]
        return pltpu.make_async_remote_copy(
            src_ref=part, dst_ref=part, send_sem=a_ss.at[m // 2], recv_sem=a_rs.at[h, c, m // 2],
            device_id={"tensor": flipped(tme, m)}, device_id_type=MESH,
        )

    def f_copy_from(h, c, m):
        part = ag.at[h, c, group_head(flipped(flipped(tme, 1), m))]
        return pltpu.make_async_remote_copy(
            src_ref=part, dst_ref=part, send_sem=f_ss.at[m // 2], recv_sem=f_rs.at[h, c, m // 2],
            device_id={"tensor": flipped(tme, 1)}, device_id_type=MESH,
        )

    turn = 128 if feats % 128 == 0 else feats

    def out_copy(c):
        return pltpu.make_async_copy(out_vm.at[c], out_hbm.at[:, tokens(c)], out_sem.at[c])

    def settle(h, c):
        a_copy_from(h, c, 1).wait_recv()
        for m in others:
            f_copy_from(h, c, m).wait_recv()

    def project(parts, c):
        out = acc[c] if heads - 1 in parts and heads > 1 else None
        for h in parts:
            term = jnp.dot(wt[h], ag[h, c], preferred_element_type=jnp.float32)
            out = term if out is None else out + term
        if heads - 1 in parts:
            out_vm[c] = out.astype(out_vm.dtype)
        else:
            acc[c] = out

    def turn_weights(i, carry):
        at = pl.ds(pl.multiple_of(i * turn, turn), turn) if turn < feats else slice(None)
        for t in range(groups):
            for h in range(heads):
                rows = slice((t * heads + h) * head, (t * heads + h + 1) * head)
                wt[h, at, t * head:(t + 1) * head] = wg[rows, at].T
        return carry

    for h in range(heads - 1):
        for j in range(n - 1):
            early_stage(h, j)
            if j < n - 2:
                q_far(h + 1, half, j)
                if j < n - 3:
                    q_far(h + 1, 1 - half, j + 1)
            early_rest(h, j)
        own_partial(h)

    h = heads - 1
    for j in range(n - 1):
        last_stage(h, j)
        if j == n - 3:
            for early in range(heads - 1):
                own_final(early)
            for copy in w_copies:
                copy.wait()
            own_w.wait()
            lax.fori_loop(0, feats // turn, turn_weights, 0)
    for early in range(heads - 1):
        loop(functools.partial(forward, early))

    def project_early(c):
        for early in range(heads - 1):
            settle(early, c)
        project(range(heads - 1), c)

    own_stage(h)
    lag = 2

    def between(c):
        project_early(c)

        @pl.when(c >= lag)
        def _():
            forward(h, c - lag)

    loop(between)

    def finish(c):
        @pl.when(c < lag)
        def _():
            forward(h, c + chunks - lag)

        settle(h, c)
        project([h], c)
        out_copy(c).start()

    loop(finish)

    def drain(part, sem):
        pltpu.make_async_copy(part, part, sem).wait()

    drain(tab_in.at[pl.ds(0, peers - 1)], t_ss)
    drain(sk, k_ss)
    drain(sv, v_ss)

    for right in (1, 0):
        for k in range(n):
            source = z - k * (2 * right - 1)

            @pl.when(jnp.logical_and(behind(right) >= k, ahead(right) > 0))
            def _():
                drain(qb.at[source], q_ss.at[right, source])

    drain(o_out.at[:, pl.ds(0, n - 1)], o_ss)
    drain(s_out.at[:, pl.ds(0, n - 1)], s_ss)
    for m in others + [1]:
        drain(ag.at[:, :, group_head(tme)], a_ss.at[m // 2])
    for m in others:
        drain(ag.at[:, :, group_head(tme)], f_ss.at[m // 2])
    for c in range(chunks):
        out_copy(c).wait()


def shards(
    queries, keys, values, mem_keys, mem_values, gate_bias, out_weight, retrieved, block_slot
):
    tok, width = queries.shape
    heads = gate_bias.shape[0]
    head = width // heads
    peers = lax.axis_size("dp")
    groups = lax.axis_size("tensor")
    n = peers // 2
    local_blocks = mem_keys.shape[0] // BLOCK
    feats = out_weight.shape[1] // groups
    chunks = tok // CHUNK
    sliced = feats % 128 == 0
    weight = out_weight
    if not sliced:
        weight = out_weight.reshape(width, groups, feats).transpose(1, 0, 2)
    blocked = (local_blocks, BLOCK, width)
    bf16, f32 = jnp.bfloat16, jnp.float32
    landing = pltpu.VMEM((2 * UNIQ_CAP, BLOCK, head), bf16)
    landings = tuple(tuple(landing for _ in range(n)) for _ in range(heads))
    wide = block_slot.shape[0]
    stat_rows = 2 * CHUNK // BLOCK
    dma = pltpu.SemaphoreType.DMA
    smem = pl.BlockSpec(memory_space=pltpu.SMEM)
    any_spec = pl.BlockSpec(memory_space=pltpu.HBM)
    return pl.pallas_call(
        functools.partial(layer_kernel, n, groups, heads, peers <= 8, sliced),
        out_shape=jax.ShapeDtypeStruct((feats, tok), bf16),
        in_specs=[smem] * 3 + [any_spec] * 6,
        out_specs=pl.BlockSpec(memory_space=pl.ANY),
        scratch_shapes=[
            pltpu.VMEM((n, heads, tok, head), bf16),
            pltpu.VMEM((heads, tok, head), bf16),
            pltpu.VMEM((tok, width), bf16),
            pltpu.VMEM((heads, tok // BLOCK, head, BLOCK), bf16),
            pltpu.VMEM((heads, local_blocks, BLOCK, head), bf16),
            pltpu.VMEM(blocked, bf16),
            pltpu.VMEM((heads, local_blocks, head, BLOCK), bf16),
            pltpu.VMEM((heads, n, UNIQ_CAP, BLOCK, head), bf16),
            pltpu.VMEM((heads, n, UNIQ_CAP, head, BLOCK), bf16),
            landings,
            landings,
            pltpu.VMEM((heads, tok // BLOCK, head, BLOCK), f32),
            pltpu.VMEM((n, chunks, head, CHUNK), f32),
            pltpu.VMEM((n, chunks, stat_rows, BLOCK), f32),
            pltpu.VMEM((heads, n, chunks, head, CHUNK), bf16),
            pltpu.VMEM((heads, n, chunks, stat_rows, BLOCK), f32),
            pltpu.VMEM((2, n, heads, chunks, head, CHUNK), bf16),
            pltpu.VMEM((2, n, heads, chunks, stat_rows, BLOCK), f32),
            pltpu.VMEM((groups * width, feats), bf16),
            pltpu.VMEM((heads, feats, groups * head), bf16),
            pltpu.VMEM((chunks, feats, CHUNK), f32),
            pltpu.VMEM((heads, chunks, groups * head, CHUNK), bf16),
            pltpu.VMEM((chunks, feats, CHUNK), bf16),
            pltpu.VMEM((peers, 8, wide), jnp.int32),
            pltpu.SMEM((peers, 8, wide), jnp.int32),
            dma((3 * heads + 2,)),
            dma(()),
            dma(()),
            dma((chunks,)),
            dma(()),
            dma((peers,)),
            dma((2, n)),
            dma((n, heads, chunks)),
            dma(()),
            dma((heads, n)),
            dma(()),
            dma((heads, n)),
            dma(()),
            dma((2, n, heads, chunks)),
            dma(()),
            dma((2, n, heads, chunks)),
            dma((groups,)),
            dma((groups,)),
            dma((groups // 2,)),
            dma((heads, chunks, groups // 2)),
            dma((groups // 2,)),
            dma((heads, chunks, groups // 2)),
        ],
        compiler_params=pltpu.CompilerParams(
            collective_id=0, has_side_effects=True, vmem_limit_bytes=(49 if peers <= 8 else 62) * 2**20
        ),
        name="memory_layer",
    )(
        *[
            pltpu.with_memory_space_constraint(operand, pltpu.HBM)
            for operand in (
                retrieved.T, block_slot, gate_bias, queries, keys, values,
                mem_keys.reshape(blocked), mem_values.reshape(blocked), weight,
            )
        ]
    )


def solution(mesh):
    in_specs = (
        P("dp", "tensor"),
        P("dp", "tensor"),
        P("dp", "tensor"),
        P("dp", "tensor"),
        P("dp", "tensor"),
        P("tensor"),
        P("tensor", None),
        P("dp", None),
        P(),
    )
    out_specs = P("tensor", "dp")
    return jax.shard_map(shards, mesh=mesh, in_specs=in_specs, out_specs=out_specs, check_vma=False)
```

```python
import functools
import math

import jax
import jax.numpy as jnp
from jax import lax
from jax.experimental import pallas as pl
from jax.experimental.pallas import tpu as pltpu
from jax.sharding import PartitionSpec as P

BLOCK = 128
SEG = 512
TOPK = 4
UNIQ_CAP = 4
CHUNK = 256
NEG = -3.0e38
MESH = pl.DeviceIdType.MESH
NT = (((1,), (1,)), ((), ()))
RANK_ROW = UNIQ_CAP
SLOT_ROW = UNIQ_CAP + 1


def flipped(index, mask):
    bit = 1
    result = index
    while bit <= mask:
        if mask & bit:
            result = result + bit * (1 - 2 * (lax.rem(lax.div(index, bit), 2)))
        bit *= 2
    return result


def at_least(value, bound):
    return lax.div(value - bound + 64, 64)


def layer_kernel(
    n, groups, heads, rung_minor, sliced,
    ret_ref, slot_ref, gate_ref, q_hbm, k_hbm, v_hbm, mk_hbm, mv_hbm, w_hbm,
    out_hbm,
    qb, kl, vl, vt, kown, vraw, vown, sk, sv, land_k, land_v, loc, po, st, probs,
    o_out, s_out, o_in, s_in, wg, wt, acc, ag, out_vm, tab_in, tab_sm,
    in_sem, smem_sem, own_w_sem, out_sem, t_ss, t_rs, q_ss, q_rs, k_ss, k_rs, v_ss, v_rs,
    o_ss, o_rs, s_ss, s_rs, w_ss, w_rs, a_ss, a_rs, f_ss, f_rs,
):
    me = lax.axis_index("dp")
    tme = lax.axis_index("tensor")
    peers = 2 * n
    local_blocks = kown.shape[1]
    chunks, head = ag.shape[1], kl.shape[2]
    tok = kl.shape[1]
    feats = wg.shape[1]
    scale = head ** -0.5 * math.log2(math.e)

    def split(index):
        if rung_minor:
            return lax.div(index, 2), lax.rem(index, 2)
        return lax.rem(index, n), lax.div(index, n)

    def join(line, rung):
        return line * 2 + rung if rung_minor else rung * n + line

    z, x = split(me)
    mirror = join(z, 1 - x)
    half = lax.div(2 * z, n)
    near = z * (1 - half) + (n - 1 - z) * half

    def stage_flow(h, j):
        both = at_least(2 * near, j + 1)
        tau = both * (j // 2) + (1 - both) * (j - near)
        primary = both * (1 - j % 2) + (1 - both)
        right = primary * (1 - half) + (1 - primary) * half
        if h < heads - 1:
            return right, z + (tau + 1) * (2 * right - 1)
        return right, right * (n - 1 - tau) + (1 - right) * tau

    loads = []

    def load(src, dst):
        copy = pltpu.make_async_copy(src, dst, in_sem.at[len(loads)])
        copy.start()
        loads.append(copy)

    def cols(h):
        return pl.ds(h * head, head)

    for h in range(heads):
        load(q_hbm.at[:, cols(h)], qb.at[z, h])
    for h in range(heads):
        load(mk_hbm.at[:, :, cols(h)], kown.at[h])
    load(mv_hbm, vraw)
    for h in range(heads):
        load(k_hbm.at[:, cols(h)], kl.at[h])
    load(v_hbm, vl)

    barrier = pltpu.get_barrier_semaphore()
    for m in range(1, peers):
        pl.semaphore_signal(barrier, inc=1, device_id={"dp": flipped(me, m)}, device_id_type=MESH)
    for m in range(1, groups):
        pl.semaphore_signal(
            barrier, inc=1, device_id={"tensor": flipped(tme, m)}, device_id_type=MESH
        )

    wide = tab_in.shape[2]
    lane = lax.broadcasted_iota(jnp.int32, (8, wide), 1)
    sub = lax.broadcasted_iota(jnp.int32, (8, wide), 0)
    inner = lax.rem(lane, local_blocks)
    slots = jnp.zeros((8, wide), jnp.int32)
    present = jnp.zeros((8, wide), jnp.int32)
    for b in range(tok // BLOCK):
        for i in range(TOPK):
            slot = slot_ref[ret_ref[i, b]]
            slots = jnp.where(lane == b * TOPK + i, slot, slots)
            present = jnp.where(lane == slot, 1, present)
    rank = present
    shift = 1
    while shift < local_blocks:
        rank = rank + jnp.where(inner >= shift, pltpu.roll(rank, shift, 1), 0)
        shift *= 2
    rank = rank - present
    wanted = jnp.where((present == 1) & (rank == sub), inner, 0)
    shift = local_blocks // 2
    while shift >= 1:
        wanted = jnp.maximum(wanted, pltpu.roll(wanted, wide - shift, 1))
        shift //= 2
    table = jnp.where(sub < UNIQ_CAP, wanted, jnp.where(sub == RANK_ROW, rank, slots))
    tab_in[me] = table

    pl.semaphore_wait(barrier, peers - 1 + groups - 1)

    tables = []
    for m in range(1, peers):
        copy = pltpu.make_async_remote_copy(
            src_ref=tab_in.at[me], dst_ref=tab_in.at[me], send_sem=t_ss,
            recv_sem=t_rs.at[m], device_id={"dp": flipped(me, m)}, device_id_type=MESH,
        )
        copy.start()
        tables.append(copy)

    def tokens(c):
        return pl.ds(pl.multiple_of(c * CHUNK, CHUNK), CHUNK)

    def q_copy(right, source, h, c):
        part = qb.at[source, h, tokens(c)]
        return pltpu.make_async_remote_copy(
            src_ref=part, dst_ref=part, send_sem=q_ss.at[right, source],
            recv_sem=q_rs.at[source, h, c],
            device_id={"dp": join(z + 2 * right - 1, x)}, device_id_type=MESH,
        )

    def behind(right):
        return right * z + (1 - right) * (n - 1 - z)

    def ahead(right):
        return n - 1 - behind(right)

    def q_own(h, right, when):
        @pl.when(jnp.logical_and(ahead(right) > 0, when))
        def _():
            for c in range(chunks):
                q_copy(right, z, h, c).start()

    def q_pass(h, right, source, valid, c):
        @pl.when(jnp.logical_and(ahead(right) > 0, valid))
        def _():
            q_copy(right, source, h, c).wait_recv()
            q_copy(right, source, h, c).start()

    def q_near(k, c):
        for right in (1 - half, half):
            q_pass(0, right, z - k * (2 * right - 1), behind(right) >= k, c)

    def q_far(h, right, tau):
        source = right * tau + (1 - right) * (n - 1 - tau)

        def step(c, carry):
            q_pass(h, right, source, behind(right) > tau, c)
            return carry

        lax.fori_loop(0, chunks, step, 0)
        q_own(h, right, behind(right) == tau + 1)

    def loop(fn):
        def step(c, carry):
            fn(c)
            return carry

        lax.fori_loop(0, chunks, step, 0)

    def q_end(h, d):
        @pl.when(near == 0)
        def _():
            loop(lambda c: q_copy(half, d, h, c).wait_recv())

    for h in range(heads):
        loads[h].wait()
    for h in range(min(heads, 2)):
        for right in (1 - half, half):
            q_own(h, right, behind(right) == 0 if h else True)

    def weight_part(t):
        if sliced:
            return w_hbm.at[:, pl.ds(pl.multiple_of(t * feats, 128), feats)]
        return w_hbm.at[t]

    def group_rows(t):
        return pl.ds(pl.multiple_of(t * heads * head, 128), heads * head)

    w_copies = []
    for m in range(1, groups):
        peer = flipped(tme, m)
        copy = pltpu.make_async_remote_copy(
            src_ref=weight_part(peer), dst_ref=wg.at[group_rows(tme)],
            send_sem=w_ss.at[m], recv_sem=w_rs.at[m], device_id={"tensor": peer},
            device_id_type=MESH,
        )
        copy.start()
        w_copies.append(copy)
    own_w = pltpu.make_async_copy(weight_part(tme), wg.at[group_rows(tme)], own_w_sem)
    own_w.start()

    for h in range(heads):
        loads[heads + h].wait()
    loads[2 * heads].wait()

    def turn_values(i, carry):
        for h in range(heads):
            vown[h, i] = vraw[i, :, h * head:(h + 1) * head].T
        return carry

    lax.fori_loop(0, local_blocks, turn_values, 0)

    def turn_local(i, carry):
        rows = pl.ds(pl.multiple_of(i * BLOCK, BLOCK), BLOCK)
        for h in range(heads):
            vt[h, i] = vl[rows, h * head:(h + 1) * head].T
        return carry


    def gate(h, width):
        bias = jnp.full((1, width), gate_ref[h], jnp.float32)
        return 1.0 / (1.0 + jnp.exp(-bias))

    blocks_seg = SEG // BLOCK
    per_chunk = CHUNK // BLOCK

    def local_segment(u, carry):
        s, h = lax.div(u, heads), lax.rem(u, heads)
        first = s * blocks_seg
        key_row = lax.broadcasted_iota(jnp.int32, (BLOCK, BLOCK), 0)
        query_col = lax.broadcasted_iota(jnp.int32, (BLOCK, BLOCK), 1)
        keep = 1.0 - gate(h, BLOCK)
        for i in range(blocks_seg):
            span = (i + 1) * BLOCK
            base = pl.multiple_of(s * SEG, SEG)
            scores = lax.dot_general(
                kl[h, pl.ds(base, span)], qb[z, h, pl.ds(base + i * BLOCK, BLOCK)], NT,
                preferred_element_type=jnp.float32,
            )
            last = jnp.where(key_row <= query_col, scores[i * BLOCK:], -jnp.inf)
            scores = last if i == 0 else jnp.concatenate([scores[:i * BLOCK], last], axis=0)
            top = jnp.max(scores, axis=0, keepdims=True)
            weights = jnp.exp2((scores - top) * scale)
            total = jnp.sum(weights, axis=0, keepdims=True)
            vals = jnp.concatenate([vt[h, first + g] for g in range(i + 1)], axis=1)
            out = jnp.dot(
                vals, weights.astype(jnp.bfloat16), preferred_element_type=jnp.float32
            )
            loc[h, first + i] = out * (keep / total)
        return carry

    def local_attention():
        for copy in loads[2 * heads + 1:]:
            copy.wait()
        lax.fori_loop(0, tok // BLOCK, turn_local, 0)
        lax.fori_loop(0, tok // SEG * heads, local_segment, 0)

    for copy in tables:
        copy.wait_recv()
    to_smem = pltpu.make_async_copy(tab_in, tab_sm, smem_sem)
    to_smem.start()
    to_smem.wait()

    ships = {}
    for h in range(heads):
        for j in range(n):
            d = z if j == n - 1 else stage_flow(h, j)[1]
            reader = join(d, 1 - x)
            for key, own, send, land, ss, rs in (
                ("k", kown, sk, land_k, k_ss, k_rs), ("v", vown, sv, land_v, v_ss, v_rs)
            ):
                for c in range(UNIQ_CAP):
                    send[h, j, c] = own[h, tab_sm[reader, c, me * local_blocks]]
                copy = pltpu.make_async_remote_copy(
                    src_ref=send.at[h, j], dst_ref=land[h][j].at[pl.ds(UNIQ_CAP, UNIQ_CAP)],
                    send_sem=ss, recv_sem=rs.at[h, j], device_id={"dp": mirror},
                    device_id_type=MESH,
                )
                copy.start()
                ships[key, h, j] = copy

    loop(functools.partial(q_near, 1))
    local_attention()
    for k in range(2, n - 1):
        loop(functools.partial(q_near, k))
    if heads > 1:
        q_far(1, 1 - half, 0)

    def places_of(d, b):
        owner_at = join(d, x)
        places, valid = [], []
        for i in range(TOPK):
            slot = tab_sm[owner_at, SLOT_ROW, b * TOPK + i]
            line, rung = split(lax.div(slot, local_blocks))
            side = lax.rem(rung + x, 2)
            places.append(side * UNIQ_CAP + tab_sm[owner_at, RANK_ROW, slot])
            valid.append(line == z)
        return places, valid

    def block_weights(h, j, d, b):
        places, valid = places_of(d, b)
        keys = jnp.concatenate([land_k[h][j][p] for p in places], axis=0)
        rows = pl.ds(pl.multiple_of(b * BLOCK, BLOCK), BLOCK)
        scores = lax.dot_general(keys, qb[d, h, rows], NT, preferred_element_type=jnp.float32)
        scores = jnp.concatenate(
            [
                jnp.where(valid[i], scores[i * BLOCK:(i + 1) * BLOCK], NEG)
                for i in range(TOPK)
            ],
            axis=0,
        )
        top = jnp.max(scores, axis=0, keepdims=True)
        weights = jnp.exp2((scores - top) * scale)
        total = jnp.sum(weights, axis=0, keepdims=True)
        return weights.astype(jnp.bfloat16), top, total

    def block_values(h, j, d, b, weights):
        places, _ = places_of(d, b)
        vals = jnp.concatenate([land_v[h][j][p] for p in places], axis=1)
        return jnp.dot(vals, weights, preferred_element_type=jnp.float32)

    def lanes(blk):
        return slice(blk * BLOCK, (blk + 1) * BLOCK)

    def partial_chunk(h, j, d, c):
        tops, totals = [], []
        for blk in range(per_chunk):
            b = c * per_chunk + blk
            weights, top, total = block_weights(h, j, d, b)
            po[d, c, :, lanes(blk)] = block_values(h, j, d, b, weights)
            tops.append(top)
            totals.append(total)
        st[d, c] = jnp.concatenate(tops + totals, axis=0)

    def own_weights(h, c):
        tops, totals = [], []
        for blk in range(per_chunk):
            b = c * per_chunk + blk
            probs[b], top, total = block_weights(h, n - 1, z, b)
            tops.append(top)
            totals.append(total)
        st[z, c] = jnp.concatenate(tops + totals, axis=0)

    def own_values(h, c):
        for blk in range(per_chunk):
            b = c * per_chunk + blk
            po[z, c, :, lanes(blk)] = block_values(h, n - 1, z, b, probs[b])

    def merged(right, d, h, c):
        o_copy(right, d, h, c).wait_recv()
        s_copy(right, d, h, c).wait_recv()
        stats, stats_in = st[d, c], s_in[right, d, h, c]
        top, total = stats[:per_chunk], stats[per_chunk:]
        top_in, total_in = stats_in[:per_chunk], stats_in[per_chunk:]
        new = jnp.maximum(top, top_in)
        mine = jnp.exp2((top - new) * scale)
        theirs = jnp.exp2((top_in - new) * scale)
        parts = [
            po[d, c, :, lanes(blk)] * mine[blk:blk + 1]
            + o_in[right, d, h, c, :, lanes(blk)].astype(jnp.float32) * theirs[blk:blk + 1]
            for blk in range(per_chunk)
        ]
        stats = jnp.concatenate([new, total * mine + total_in * theirs], axis=0)
        return jnp.concatenate(parts, axis=1), stats

    def o_copy(right, d, h, c):
        return pltpu.make_async_remote_copy(
            src_ref=o_out.at[h, d, c], dst_ref=o_in.at[right, d, h, c],
            send_sem=o_ss, recv_sem=o_rs.at[right, d, h, c],
            device_id={"dp": join(z + 2 * right - 1, x)}, device_id_type=MESH,
        )

    def s_copy(right, d, h, c):
        return pltpu.make_async_remote_copy(
            src_ref=s_out.at[h, d, c], dst_ref=s_in.at[right, d, h, c],
            send_sem=s_ss, recv_sem=s_rs.at[right, d, h, c],
            device_id={"dp": join(z + 2 * right - 1, x)}, device_id_type=MESH,
        )

    def group_head(t):
        return pl.ds(pl.multiple_of(t * head, 128), head)

    def a_copy(h, c, m):
        part = ag.at[h, c, group_head(tme)]
        return pltpu.make_async_remote_copy(
            src_ref=part, dst_ref=part, send_sem=a_ss.at[m // 2], recv_sem=a_rs.at[h, c, m // 2],
            device_id={"tensor": flipped(tme, m)}, device_id_type=MESH,
        )

    def f_copy(h, c, m):
        part = ag.at[h, c, group_head(flipped(tme, m))]
        return pltpu.make_async_remote_copy(
            src_ref=part, dst_ref=part, send_sem=f_ss.at[m // 2], recv_sem=f_rs.at[h, c, m // 2],
            device_id={"tensor": flipped(tme, 1)}, device_id_type=MESH,
        )

    others = list(range(2, groups, 2))

    def arrive_part(key, own, land, h, j, d):
        ships[key, h, j].wait_recv()
        for c in range(UNIQ_CAP):
            land[h][j][c] = own[h, tab_sm[join(d, x), c, me * local_blocks]]

    def arrive(h, j, d):
        arrive_part("k", kown, land_k, h, j, d)
        arrive_part("v", vown, land_v, h, j, d)

    def pass_on(h, right, d, c):
        starts = behind(right) == 0

        @pl.when(starts)
        def _():
            o_out[h, d, c] = po[d, c].astype(o_out.dtype)
            s_out[h, d, c] = st[d, c]

        @pl.when(jnp.logical_not(starts))
        def _():
            out, stats = merged(right, d, h, c)
            o_out[h, d, c] = out.astype(o_out.dtype)
            s_out[h, d, c] = stats

        o_copy(right, d, h, c).start()
        s_copy(right, d, h, c).start()

    def last_stage(h, j):
        right, d = stage_flow(h, j)
        arrive(h, j, d)
        q_end(h, d)

        def chunk(c, carry):
            partial_chunk(h, j, d, c)
            pass_on(h, right, d, c)
            return carry

        lax.fori_loop(0, chunks, chunk, 0)

    def due(j, right):
        d = right * (j + 1) + (1 - right) * (n - 2 - j)
        return d, right * (d - z) + (1 - right) * (z - d) > 0

    def early_stage(h, j):
        d = stage_flow(h, j)[1]
        arrive(h, j, d)
        q_end(h, d)
        first, passes = due(j, 1 - half)

        def chunk(c, carry):
            partial_chunk(h, j, d, c)

            @pl.when(passes)
            def _():
                pass_on(h, 1 - half, first, c)

            return carry

        lax.fori_loop(0, chunks, chunk, 0)

    def early_rest(h, j):
        second, passes = due(j, half)

        @pl.when(passes)
        def _():
            def chunk(c, carry):
                pass_on(h, half, second, c)
                return carry

            lax.fori_loop(0, chunks, chunk, 0)

    def own_partial(h):
        arrive(h, n - 1, z)
        loop(lambda c: partial_chunk(h, n - 1, z, c))

    def own_final(h):
        loop(functools.partial(finish_chunk, h))

    def own_stage(h):
        arrive_part("k", kown, land_k, h, n - 1, z)
        loop(functools.partial(own_weights, h))
        arrive_part("v", vown, land_v, h, n - 1, z)

        def chunk(c):
            own_values(h, c)
            finish_chunk(h, c)

        loop(chunk)

    def finish_chunk(h, c):
        for right in (1 - half, half):
            @pl.when(behind(right) > 0)
            def _():
                po[z, c], st[z, c] = merged(right, z, h, c)

        for blk in range(per_chunk):
            weight = gate(h, BLOCK) / st[z, c, per_chunk + blk:per_chunk + blk + 1]
            result = po[z, c, :, lanes(blk)] * weight + loc[h, c * per_chunk + blk]
            ag[h, c, group_head(tme), lanes(blk)] = result.astype(ag.dtype)
        for m in others + [1]:
            a_copy(h, c, m).start()

    def forward(h, c):
        for m in others:
            a_copy_from(h, c, m).wait_recv()
            f_copy(h, c, m).start()

    def a_copy_from(h, c, m):
        part = ag.at[h, c, group_head(flipped(tme, m))]
        return pltpu.make_async_remote_copy(
            src_ref=part, dst_ref=part, send_sem=a_ss.at[m // 2], recv_sem=a_rs.at[h, c, m // 2],
            device_id={"tensor": flipped(tme, m)}, device_id_type=MESH,
        )

    def f_copy_from(h, c, m):
        part = ag.at[h, c, group_head(flipped(flipped(tme, 1), m))]
        return pltpu.make_async_remote_copy(
            src_ref=part, dst_ref=part, send_sem=f_ss.at[m // 2], recv_sem=f_rs.at[h, c, m // 2],
            device_id={"tensor": flipped(tme, 1)}, device_id_type=MESH,
        )

    turn = 128 if feats % 128 == 0 else feats

    def out_copy(c):
        return pltpu.make_async_copy(out_vm.at[c], out_hbm.at[:, tokens(c)], out_sem.at[c])

    def settle(h, c):
        a_copy_from(h, c, 1).wait_recv()
        for m in others:
            f_copy_from(h, c, m).wait_recv()

    def project(parts, c):
        out = acc[c] if heads - 1 in parts and heads > 1 else None
        for h in parts:
            term = jnp.dot(wt[h], ag[h, c], preferred_element_type=jnp.float32)
            out = term if out is None else out + term
        if heads - 1 in parts:
            out_vm[c] = out.astype(out_vm.dtype)
        else:
            acc[c] = out

    def turn_weights(i, carry):
        at = pl.ds(pl.multiple_of(i * turn, turn), turn) if turn < feats else slice(None)
        for t in range(groups):
            for h in range(heads):
                rows = slice((t * heads + h) * head, (t * heads + h + 1) * head)
                wt[h, at, t * head:(t + 1) * head] = wg[rows, at].T
        return carry

    for h in range(heads - 1):
        for j in range(n - 1):
            early_stage(h, j)
            if j < n - 2:
                q_far(h + 1, half, j)
                if j < n - 3:
                    q_far(h + 1, 1 - half, j + 1)
            early_rest(h, j)
        own_partial(h)

    h = heads - 1
    for j in range(n - 1):
        last_stage(h, j)
        if j == n - 3:
            for early in range(heads - 1):
                own_final(early)
            for copy in w_copies:
                copy.wait()
            own_w.wait()
            lax.fori_loop(0, feats // turn, turn_weights, 0)
    for early in range(heads - 1):
        loop(functools.partial(forward, early))

    def project_early(c):
        for early in range(heads - 1):
            settle(early, c)
        project(range(heads - 1), c)

    own_stage(h)
    lag = 2

    def between(c):
        project_early(c)

        @pl.when(c >= lag)
        def _():
            forward(h, c - lag)

    loop(between)

    def finish(c):
        @pl.when(c < lag)
        def _():
            forward(h, c + chunks - lag)

        settle(h, c)
        project([h], c)
        out_copy(c).start()

    loop(finish)

    def drain(part, sem):
        pltpu.make_async_copy(part, part, sem).wait()

    drain(tab_in.at[pl.ds(0, peers - 1)], t_ss)
    drain(sk, k_ss)
    drain(sv, v_ss)

    for right in (1, 0):
        for k in range(n):
            source = z - k * (2 * right - 1)

            @pl.when(jnp.logical_and(behind(right) >= k, ahead(right) > 0))
            def _():
                drain(qb.at[source], q_ss.at[right, source])

    drain(o_out.at[:, pl.ds(0, n - 1)], o_ss)
    drain(s_out.at[:, pl.ds(0, n - 1)], s_ss)
    for m in others + [1]:
        drain(ag.at[:, :, group_head(tme)], a_ss.at[m // 2])
    for m in others:
        drain(ag.at[:, :, group_head(tme)], f_ss.at[m // 2])
    for c in range(chunks):
        out_copy(c).wait()


def shards(
    queries, keys, values, mem_keys, mem_values, gate_bias, out_weight, retrieved, block_slot
):
    tok, width = queries.shape
    heads = gate_bias.shape[0]
    head = width // heads
    peers = lax.axis_size("dp")
    groups = lax.axis_size("tensor")
    n = peers // 2
    local_blocks = mem_keys.shape[0] // BLOCK
    feats = out_weight.shape[1] // groups
    chunks = tok // CHUNK
    sliced = feats % 128 == 0
    weight = out_weight
    if not sliced:
        weight = out_weight.reshape(width, groups, feats).transpose(1, 0, 2)
    blocked = (local_blocks, BLOCK, width)
    bf16, f32 = jnp.bfloat16, jnp.float32
    landing = pltpu.VMEM((2 * UNIQ_CAP, BLOCK, head), bf16)
    landings = tuple(tuple(landing for _ in range(n)) for _ in range(heads))
    wide = block_slot.shape[0]
    stat_rows = 2 * CHUNK // BLOCK
    dma = pltpu.SemaphoreType.DMA
    smem = pl.BlockSpec(memory_space=pltpu.SMEM)
    any_spec = pl.BlockSpec(memory_space=pltpu.HBM)
    return pl.pallas_call(
        functools.partial(layer_kernel, n, groups, heads, peers <= 8, sliced),
        out_shape=jax.ShapeDtypeStruct((feats, tok), bf16),
        in_specs=[smem] * 3 + [any_spec] * 6,
        out_specs=pl.BlockSpec(memory_space=pl.ANY),
        scratch_shapes=[
            pltpu.VMEM((n, heads, tok, head), bf16),
            pltpu.VMEM((heads, tok, head), bf16),
            pltpu.VMEM((tok, width), bf16),
            pltpu.VMEM((heads, tok // BLOCK, head, BLOCK), bf16),
            pltpu.VMEM((heads, local_blocks, BLOCK, head), bf16),
            pltpu.VMEM(blocked, bf16),
            pltpu.VMEM((heads, local_blocks, head, BLOCK), bf16),
            pltpu.VMEM((heads, n, UNIQ_CAP, BLOCK, head), bf16),
            pltpu.VMEM((heads, n, UNIQ_CAP, head, BLOCK), bf16),
            landings,
            landings,
            pltpu.VMEM((heads, tok // BLOCK, head, BLOCK), f32),
            pltpu.VMEM((n, chunks, head, CHUNK), f32),
            pltpu.VMEM((n, chunks, stat_rows, BLOCK), f32),
            pltpu.VMEM((tok // BLOCK, TOPK * BLOCK, BLOCK), bf16),
            pltpu.VMEM((heads, n, chunks, head, CHUNK), bf16),
            pltpu.VMEM((heads, n, chunks, stat_rows, BLOCK), f32),
            pltpu.VMEM((2, n, heads, chunks, head, CHUNK), bf16),
            pltpu.VMEM((2, n, heads, chunks, stat_rows, BLOCK), f32),
            pltpu.VMEM((groups * width, feats), bf16),
            pltpu.VMEM((heads, feats, groups * head), bf16),
            pltpu.VMEM((chunks, feats, CHUNK), f32),
            pltpu.VMEM((heads, chunks, groups * head, CHUNK), bf16),
            pltpu.VMEM((chunks, feats, CHUNK), bf16),
            pltpu.VMEM((peers, 8, wide), jnp.int32),
            pltpu.SMEM((peers, 8, wide), jnp.int32),
            dma((3 * heads + 2,)),
            dma(()),
            dma(()),
            dma((chunks,)),
            dma(()),
            dma((peers,)),
            dma((2, n)),
            dma((n, heads, chunks)),
            dma(()),
            dma((heads, n)),
            dma(()),
            dma((heads, n)),
            dma(()),
            dma((2, n, heads, chunks)),
            dma(()),
            dma((2, n, heads, chunks)),
            dma((groups,)),
            dma((groups,)),
            dma((groups // 2,)),
            dma((heads, chunks, groups // 2)),
            dma((groups // 2,)),
            dma((heads, chunks, groups // 2)),
        ],
        compiler_params=pltpu.CompilerParams(
            collective_id=0, has_side_effects=True, vmem_limit_bytes=(49 if peers <= 8 else 62) * 2**20
        ),
        name="memory_layer",
    )(
        *[
            pltpu.with_memory_space_constraint(operand, pltpu.HBM)
            for operand in (
                retrieved.T, block_slot, gate_bias, queries, keys, values,
                mem_keys.reshape(blocked), mem_values.reshape(blocked), weight,
            )
        ]
    )


def solution(mesh):
    in_specs = (
        P("dp", "tensor"),
        P("dp", "tensor"),
        P("dp", "tensor"),
        P("dp", "tensor"),
        P("dp", "tensor"),
        P("tensor"),
        P("tensor", None),
        P("dp", None),
        P(),
    )
    out_specs = P("tensor", "dp")
    return jax.shard_map(shards, mesh=mesh, in_specs=in_specs, out_specs=out_specs, check_vma=False)
```

```python
import functools
import math

import jax
import jax.numpy as jnp
from jax import lax
from jax.experimental import pallas as pl
from jax.experimental.pallas import tpu as pltpu
from jax.sharding import PartitionSpec as P

BLOCK = 128
SEG = 512
TOPK = 4
UNIQ_CAP = 4
CHUNK = 256
NEG = -3.0e38
MESH = pl.DeviceIdType.MESH
NT = (((1,), (1,)), ((), ()))
RANK_ROW = UNIQ_CAP
SLOT_ROW = UNIQ_CAP + 1


def flipped(index, mask):
    bit = 1
    result = index
    while bit <= mask:
        if mask & bit:
            result = result + bit * (1 - 2 * (lax.rem(lax.div(index, bit), 2)))
        bit *= 2
    return result


def at_least(value, bound):
    return lax.div(value - bound + 64, 64)


def layer_kernel(
    n, groups, heads, rung_minor, sliced,
    ret_ref, slot_ref, gate_ref, q_hbm, k_hbm, v_hbm, mk_hbm, mv_hbm, w_hbm,
    out_hbm,
    qb, kl, vl, vt, kown, vraw, vown, sk, sv, land_k, land_v, loc, po, st, probs,
    o_out, s_out, o_in, s_in, wg, wt, acc, ag, out_vm, tab_in, tab_sm,
    in_sem, smem_sem, own_w_sem, out_sem, t_ss, t_rs, q_ss, q_rs, k_ss, k_rs, v_ss, v_rs,
    o_ss, o_rs, s_ss, s_rs, w_ss, w_rs, a_ss, a_rs, f_ss, f_rs,
):
    me = lax.axis_index("dp")
    tme = lax.axis_index("tensor")
    peers = 2 * n
    local_blocks = kown.shape[1]
    chunks, head = ag.shape[1], kl.shape[2]
    tok = kl.shape[1]
    feats = wg.shape[1]
    scale = head ** -0.5 * math.log2(math.e)

    def split(index):
        if rung_minor:
            return lax.div(index, 2), lax.rem(index, 2)
        return lax.rem(index, n), lax.div(index, n)

    def join(line, rung):
        return line * 2 + rung if rung_minor else rung * n + line

    z, x = split(me)
    mirror = join(z, 1 - x)
    half = lax.div(2 * z, n)
    near = z * (1 - half) + (n - 1 - z) * half

    def stage_flow(h, j):
        both = at_least(2 * near, j + 1)
        tau = both * (j // 2) + (1 - both) * (j - near)
        primary = both * (1 - j % 2) + (1 - both)
        right = primary * (1 - half) + (1 - primary) * half
        if h < heads - 1:
            return right, z + (tau + 1) * (2 * right - 1)
        return right, right * (n - 1 - tau) + (1 - right) * tau

    loads = []

    def load(src, dst):
        copy = pltpu.make_async_copy(src, dst, in_sem.at[len(loads)])
        copy.start()
        loads.append(copy)

    def cols(h):
        return pl.ds(h * head, head)

    for h in range(heads):
        load(q_hbm.at[:, cols(h)], qb.at[z, h])
    for h in range(heads):
        load(mk_hbm.at[:, :, cols(h)], kown.at[h])
    load(mv_hbm, vraw)
    for h in range(heads):
        load(k_hbm.at[:, cols(h)], kl.at[h])
    load(v_hbm, vl)

    barrier = pltpu.get_barrier_semaphore()
    for m in range(1, peers):
        pl.semaphore_signal(barrier, inc=1, device_id={"dp": flipped(me, m)}, device_id_type=MESH)
    for m in range(1, groups):
        pl.semaphore_signal(
            barrier, inc=1, device_id={"tensor": flipped(tme, m)}, device_id_type=MESH
        )

    wide = tab_in.shape[2]
    lane = lax.broadcasted_iota(jnp.int32, (8, wide), 1)
    sub = lax.broadcasted_iota(jnp.int32, (8, wide), 0)
    inner = lax.rem(lane, local_blocks)
    slots = jnp.zeros((8, wide), jnp.int32)
    present = jnp.zeros((8, wide), jnp.int32)
    for b in range(tok // BLOCK):
        for i in range(TOPK):
            slot = slot_ref[ret_ref[i, b]]
            slots = jnp.where(lane == b * TOPK + i, slot, slots)
            present = jnp.where(lane == slot, 1, present)
    rank = present
    shift = 1
    while shift < local_blocks:
        rank = rank + jnp.where(inner >= shift, pltpu.roll(rank, shift, 1), 0)
        shift *= 2
    rank = rank - present
    wanted = jnp.where((present == 1) & (rank == sub), inner, 0)
    shift = local_blocks // 2
    while shift >= 1:
        wanted = jnp.maximum(wanted, pltpu.roll(wanted, wide - shift, 1))
        shift //= 2
    table = jnp.where(sub < UNIQ_CAP, wanted, jnp.where(sub == RANK_ROW, rank, slots))
    tab_in[me] = table

    pl.semaphore_wait(barrier, peers - 1 + groups - 1)

    tables = []
    for m in range(1, peers):
        copy = pltpu.make_async_remote_copy(
            src_ref=tab_in.at[me], dst_ref=tab_in.at[me], send_sem=t_ss,
            recv_sem=t_rs.at[m], device_id={"dp": flipped(me, m)}, device_id_type=MESH,
        )
        copy.start()
        tables.append(copy)

    def tokens(c):
        return pl.ds(pl.multiple_of(c * CHUNK, CHUNK), CHUNK)

    def q_copy(right, source, h, c):
        part = qb.at[source, h, tokens(c)]
        return pltpu.make_async_remote_copy(
            src_ref=part, dst_ref=part, send_sem=q_ss.at[right, source],
            recv_sem=q_rs.at[source, h, c],
            device_id={"dp": join(z + 2 * right - 1, x)}, device_id_type=MESH,
        )

    def behind(right):
        return right * z + (1 - right) * (n - 1 - z)

    def ahead(right):
        return n - 1 - behind(right)

    def q_own(h, right, when):
        @pl.when(jnp.logical_and(ahead(right) > 0, when))
        def _():
            for c in range(chunks):
                q_copy(right, z, h, c).start()

    def q_pass(h, right, source, valid, c):
        @pl.when(jnp.logical_and(ahead(right) > 0, valid))
        def _():
            q_copy(right, source, h, c).wait_recv()
            q_copy(right, source, h, c).start()

    def q_near(k, c):
        for right in (1 - half, half):
            q_pass(0, right, z - k * (2 * right - 1), behind(right) >= k, c)

    def q_far(h, right, tau):
        source = right * tau + (1 - right) * (n - 1 - tau)

        def step(c, carry):
            q_pass(h, right, source, behind(right) > tau, c)
            return carry

        lax.fori_loop(0, chunks, step, 0)
        q_own(h, right, behind(right) == tau + 1)

    def loop(fn):
        def step(c, carry):
            fn(c)
            return carry

        lax.fori_loop(0, chunks, step, 0)

    def q_end(h, d):
        @pl.when(near == 0)
        def _():
            loop(lambda c: q_copy(half, d, h, c).wait_recv())

    for h in range(heads):
        loads[h].wait()
    for h in range(min(heads, 2)):
        for right in (1 - half, half):
            q_own(h, right, behind(right) == 0 if h else True)

    def weight_part(t):
        if sliced:
            return w_hbm.at[:, pl.ds(pl.multiple_of(t * feats, 128), feats)]
        return w_hbm.at[t]

    def group_rows(t):
        return pl.ds(pl.multiple_of(t * heads * head, 128), heads * head)

    w_copies = []
    for m in range(1, groups):
        peer = flipped(tme, m)
        copy = pltpu.make_async_remote_copy(
            src_ref=weight_part(peer), dst_ref=wg.at[group_rows(tme)],
            send_sem=w_ss.at[m], recv_sem=w_rs.at[m], device_id={"tensor": peer},
            device_id_type=MESH,
        )
        copy.start()
        w_copies.append(copy)
    own_w = pltpu.make_async_copy(weight_part(tme), wg.at[group_rows(tme)], own_w_sem)
    own_w.start()

    for h in range(heads):
        loads[heads + h].wait()
    loads[2 * heads].wait()

    def turn_values(i, carry):
        for h in range(heads):
            vown[h, i] = vraw[i, :, h * head:(h + 1) * head].T
        return carry

    lax.fori_loop(0, local_blocks, turn_values, 0)

    def turn_local(i, carry):
        rows = pl.ds(pl.multiple_of(i * BLOCK, BLOCK), BLOCK)
        for h in range(heads):
            vt[h, i] = vl[rows, h * head:(h + 1) * head].T
        return carry


    def gate(h, width):
        bias = jnp.full((1, width), gate_ref[h], jnp.float32)
        return 1.0 / (1.0 + jnp.exp(-bias))

    blocks_seg = SEG // BLOCK
    per_chunk = CHUNK // BLOCK

    def local_segment(u, carry):
        s, h = lax.div(u, heads), lax.rem(u, heads)
        first = s * blocks_seg
        key_row = lax.broadcasted_iota(jnp.int32, (BLOCK, BLOCK), 0)
        query_col = lax.broadcasted_iota(jnp.int32, (BLOCK, BLOCK), 1)
        keep = 1.0 - gate(h, BLOCK)
        for i in range(blocks_seg):
            span = (i + 1) * BLOCK
            base = pl.multiple_of(s * SEG, SEG)
            scores = lax.dot_general(
                kl[h, pl.ds(base, span)], qb[z, h, pl.ds(base + i * BLOCK, BLOCK)], NT,
                preferred_element_type=jnp.float32,
            )
            last = jnp.where(key_row <= query_col, scores[i * BLOCK:], -jnp.inf)
            scores = last if i == 0 else jnp.concatenate([scores[:i * BLOCK], last], axis=0)
            top = jnp.max(scores, axis=0, keepdims=True)
            weights = jnp.exp2((scores - top) * scale)
            total = jnp.sum(weights, axis=0, keepdims=True)
            vals = jnp.concatenate([vt[h, first + g] for g in range(i + 1)], axis=1)
            out = jnp.dot(
                vals, weights.astype(jnp.bfloat16), preferred_element_type=jnp.float32
            )
            loc[h, first + i] = out * (keep / total)
        return carry

    def local_attention():
        for copy in loads[2 * heads + 1:]:
            copy.wait()
        lax.fori_loop(0, tok // BLOCK, turn_local, 0)
        lax.fori_loop(0, tok // SEG * heads, local_segment, 0)

    for copy in tables:
        copy.wait_recv()
    to_smem = pltpu.make_async_copy(tab_in, tab_sm, smem_sem)
    to_smem.start()
    to_smem.wait()

    ships = {}
    for h in range(heads):
        for j in range(n):
            d = z if j == n - 1 else stage_flow(h, j)[1]
            reader = join(d, 1 - x)
            for key, own, send, land, ss, rs in (
                ("k", kown, sk, land_k, k_ss, k_rs), ("v", vown, sv, land_v, v_ss, v_rs)
            ):
                for c in range(UNIQ_CAP):
                    send[h, j, c] = own[h, tab_sm[reader, c, me * local_blocks]]
                copy = pltpu.make_async_remote_copy(
                    src_ref=send.at[h, j], dst_ref=land[h][j].at[pl.ds(UNIQ_CAP, UNIQ_CAP)],
                    send_sem=ss, recv_sem=rs.at[h, j], device_id={"dp": mirror},
                    device_id_type=MESH,
                )
                copy.start()
                ships[key, h, j] = copy

    loop(functools.partial(q_near, 1))
    local_attention()
    for k in range(2, n - 1):
        loop(functools.partial(q_near, k))
    if heads > 1:
        q_far(1, 1 - half, 0)

    def places_of(d, b):
        owner_at = join(d, x)
        places, valid = [], []
        for i in range(TOPK):
            slot = tab_sm[owner_at, SLOT_ROW, b * TOPK + i]
            line, rung = split(lax.div(slot, local_blocks))
            side = lax.rem(rung + x, 2)
            places.append(side * UNIQ_CAP + tab_sm[owner_at, RANK_ROW, slot])
            valid.append(line == z)
        return places, valid

    def block_weights(h, j, d, b):
        places, valid = places_of(d, b)
        keys = jnp.concatenate([land_k[h][j][p] for p in places], axis=0)
        rows = pl.ds(pl.multiple_of(b * BLOCK, BLOCK), BLOCK)
        scores = lax.dot_general(keys, qb[d, h, rows], NT, preferred_element_type=jnp.float32)
        scores = jnp.concatenate(
            [
                jnp.where(valid[i], scores[i * BLOCK:(i + 1) * BLOCK], NEG)
                for i in range(TOPK)
            ],
            axis=0,
        )
        top = jnp.max(scores, axis=0, keepdims=True)
        weights = jnp.exp2((scores - top) * scale)
        total = jnp.sum(weights, axis=0, keepdims=True)
        return weights.astype(jnp.bfloat16), top, total

    def block_values(h, j, d, b, weights):
        places, _ = places_of(d, b)
        vals = jnp.concatenate([land_v[h][j][p] for p in places], axis=1)
        return jnp.dot(vals, weights, preferred_element_type=jnp.float32)

    def lanes(blk):
        return slice(blk * BLOCK, (blk + 1) * BLOCK)

    def partial_chunk(h, j, d, c):
        tops, totals = [], []
        for blk in range(per_chunk):
            b = c * per_chunk + blk
            weights, top, total = block_weights(h, j, d, b)
            po[d, c, :, lanes(blk)] = block_values(h, j, d, b, weights)
            tops.append(top)
            totals.append(total)
        st[d, c] = jnp.concatenate(tops + totals, axis=0)

    def own_weights(h, c):
        tops, totals = [], []
        for blk in range(per_chunk):
            b = c * per_chunk + blk
            probs[b], top, total = block_weights(h, n - 1, z, b)
            tops.append(top)
            totals.append(total)
        st[z, c] = jnp.concatenate(tops + totals, axis=0)

    def own_values(h, c):
        for blk in range(per_chunk):
            b = c * per_chunk + blk
            po[z, c, :, lanes(blk)] = block_values(h, n - 1, z, b, probs[b])

    def merged(right, d, h, c):
        o_copy(right, d, h, c).wait_recv()
        s_copy(right, d, h, c).wait_recv()
        stats, stats_in = st[d, c], s_in[right, d, h, c]
        top, total = stats[:per_chunk], stats[per_chunk:]
        top_in, total_in = stats_in[:per_chunk], stats_in[per_chunk:]
        new = jnp.maximum(top, top_in)
        mine = jnp.exp2((top - new) * scale)
        theirs = jnp.exp2((top_in - new) * scale)
        parts = [
            po[d, c, :, lanes(blk)] * mine[blk:blk + 1]
            + o_in[right, d, h, c, :, lanes(blk)].astype(jnp.float32) * theirs[blk:blk + 1]
            for blk in range(per_chunk)
        ]
        stats = jnp.concatenate([new, total * mine + total_in * theirs], axis=0)
        return jnp.concatenate(parts, axis=1), stats

    def o_copy(right, d, h, c):
        return pltpu.make_async_remote_copy(
            src_ref=o_out.at[h, d, c], dst_ref=o_in.at[right, d, h, c],
            send_sem=o_ss, recv_sem=o_rs.at[right, d, h, c],
            device_id={"dp": join(z + 2 * right - 1, x)}, device_id_type=MESH,
        )

    def s_copy(right, d, h, c):
        return pltpu.make_async_remote_copy(
            src_ref=s_out.at[h, d, c], dst_ref=s_in.at[right, d, h, c],
            send_sem=s_ss, recv_sem=s_rs.at[right, d, h, c],
            device_id={"dp": join(z + 2 * right - 1, x)}, device_id_type=MESH,
        )

    def group_head(t):
        return pl.ds(pl.multiple_of(t * head, 128), head)

    def a_copy(h, c, m):
        part = ag.at[h, c, group_head(tme)]
        return pltpu.make_async_remote_copy(
            src_ref=part, dst_ref=part, send_sem=a_ss.at[m // 2], recv_sem=a_rs.at[h, c, m // 2],
            device_id={"tensor": flipped(tme, m)}, device_id_type=MESH,
        )

    def f_copy(h, c, m):
        part = ag.at[h, c, group_head(flipped(tme, m))]
        return pltpu.make_async_remote_copy(
            src_ref=part, dst_ref=part, send_sem=f_ss.at[m // 2], recv_sem=f_rs.at[h, c, m // 2],
            device_id={"tensor": flipped(tme, 1)}, device_id_type=MESH,
        )

    others = list(range(2, groups, 2))

    def arrive_part(key, own, land, h, j, d):
        ships[key, h, j].wait_recv()
        for c in range(UNIQ_CAP):
            land[h][j][c] = own[h, tab_sm[join(d, x), c, me * local_blocks]]

    def arrive(h, j, d):
        arrive_part("k", kown, land_k, h, j, d)
        arrive_part("v", vown, land_v, h, j, d)

    def pass_on(h, right, d, c):
        starts = behind(right) == 0

        @pl.when(starts)
        def _():
            o_out[h, d, c] = po[d, c].astype(o_out.dtype)
            s_out[h, d, c] = st[d, c]

        @pl.when(jnp.logical_not(starts))
        def _():
            out, stats = merged(right, d, h, c)
            o_out[h, d, c] = out.astype(o_out.dtype)
            s_out[h, d, c] = stats

        o_copy(right, d, h, c).start()
        s_copy(right, d, h, c).start()

    def last_stage(h, j):
        right, d = stage_flow(h, j)
        arrive(h, j, d)
        q_end(h, d)

        def chunk(c, carry):
            partial_chunk(h, j, d, c)
            pass_on(h, right, d, c)
            return carry

        lax.fori_loop(0, chunks, chunk, 0)

    def due(j, right):
        d = right * (j + 1) + (1 - right) * (n - 2 - j)
        return d, right * (d - z) + (1 - right) * (z - d) > 0

    def early_stage(h, j):
        d = stage_flow(h, j)[1]
        arrive(h, j, d)
        q_end(h, d)
        first, passes = due(j, 1 - half)

        def chunk(c, carry):
            partial_chunk(h, j, d, c)

            @pl.when(passes)
            def _():
                pass_on(h, 1 - half, first, c)

            return carry

        lax.fori_loop(0, chunks, chunk, 0)

    def early_rest(h, j):
        second, passes = due(j, half)

        @pl.when(passes)
        def _():
            def chunk(c, carry):
                pass_on(h, half, second, c)
                return carry

            lax.fori_loop(0, chunks, chunk, 0)

    def own_partial(h):
        arrive(h, n - 1, z)
        loop(lambda c: partial_chunk(h, n - 1, z, c))

    def own_final(h):
        loop(functools.partial(finish_chunk, h))

    def own_stage(h):
        arrive_part("k", kown, land_k, h, n - 1, z)
        loop(functools.partial(own_weights, h))
        arrive_part("v", vown, land_v, h, n - 1, z)

        def chunk(c):
            own_values(h, c)
            finish_chunk(h, c)

        loop(chunk)

    def finish_chunk(h, c):
        for right in (1 - half, half):
            @pl.when(behind(right) > 0)
            def _():
                po[z, c], st[z, c] = merged(right, z, h, c)

        for blk in range(per_chunk):
            weight = gate(h, BLOCK) / st[z, c, per_chunk + blk:per_chunk + blk + 1]
            result = po[z, c, :, lanes(blk)] * weight + loc[h, c * per_chunk + blk]
            ag[h, c, group_head(tme), lanes(blk)] = result.astype(ag.dtype)
        for m in others + [1]:
            a_copy(h, c, m).start()

    def forward(h, c):
        for m in others:
            a_copy_from(h, c, m).wait_recv()
            f_copy(h, c, m).start()

    def a_copy_from(h, c, m):
        part = ag.at[h, c, group_head(flipped(tme, m))]
        return pltpu.make_async_remote_copy(
            src_ref=part, dst_ref=part, send_sem=a_ss.at[m // 2], recv_sem=a_rs.at[h, c, m // 2],
            device_id={"tensor": flipped(tme, m)}, device_id_type=MESH,
        )

    def f_copy_from(h, c, m):
        part = ag.at[h, c, group_head(flipped(flipped(tme, 1), m))]
        return pltpu.make_async_remote_copy(
            src_ref=part, dst_ref=part, send_sem=f_ss.at[m // 2], recv_sem=f_rs.at[h, c, m // 2],
            device_id={"tensor": flipped(tme, 1)}, device_id_type=MESH,
        )

    turn = 128 if feats % 128 == 0 else feats

    def out_copy(c):
        return pltpu.make_async_copy(out_vm.at[c], out_hbm.at[:, tokens(c)], out_sem.at[c])

    def settle(h, c):
        a_copy_from(h, c, 1).wait_recv()
        for m in others:
            f_copy_from(h, c, m).wait_recv()

    def project(parts, c):
        out = acc[c] if heads - 1 in parts and heads > 1 else None
        for h in parts:
            term = jnp.dot(wt[h], ag[h, c], preferred_element_type=jnp.float32)
            out = term if out is None else out + term
        if heads - 1 in parts:
            out_vm[c] = out.astype(out_vm.dtype)
        else:
            acc[c] = out

    def turn_weights(i, carry):
        at = pl.ds(pl.multiple_of(i * turn, turn), turn) if turn < feats else slice(None)
        for t in range(groups):
            for h in range(heads):
                rows = slice((t * heads + h) * head, (t * heads + h + 1) * head)
                wt[h, at, t * head:(t + 1) * head] = wg[rows, at].T
        return carry

    for h in range(heads - 1):
        for j in range(n - 1):
            early_stage(h, j)
            if j < n - 2:
                q_far(h + 1, half, j)
                if j < n - 3:
                    q_far(h + 1, 1 - half, j + 1)
            early_rest(h, j)
        own_partial(h)

    h = heads - 1
    for j in range(n - 1):
        last_stage(h, j)
        if j == max(n - 4, 0):
            for early in range(heads - 1):
                own_final(early)
        if j == n - 3:
            for copy in w_copies:
                copy.wait()
            own_w.wait()
            lax.fori_loop(0, feats // turn, turn_weights, 0)
    for early in range(heads - 1):
        loop(functools.partial(forward, early))

    def project_early(c):
        for early in range(heads - 1):
            settle(early, c)
        project(range(heads - 1), c)

    own_stage(h)
    lag = 2

    def between(c):
        project_early(c)

        @pl.when(c >= lag)
        def _():
            forward(h, c - lag)

    loop(between)

    def finish(c):
        @pl.when(c < lag)
        def _():
            forward(h, c + chunks - lag)

        settle(h, c)
        project([h], c)
        out_copy(c).start()

    loop(finish)

    def drain(part, sem):
        pltpu.make_async_copy(part, part, sem).wait()

    drain(tab_in.at[pl.ds(0, peers - 1)], t_ss)
    drain(sk, k_ss)
    drain(sv, v_ss)

    for right in (1, 0):
        for k in range(n):
            source = z - k * (2 * right - 1)

            @pl.when(jnp.logical_and(behind(right) >= k, ahead(right) > 0))
            def _():
                drain(qb.at[source], q_ss.at[right, source])

    drain(o_out.at[:, pl.ds(0, n - 1)], o_ss)
    drain(s_out.at[:, pl.ds(0, n - 1)], s_ss)
    for m in others + [1]:
        drain(ag.at[:, :, group_head(tme)], a_ss.at[m // 2])
    for m in others:
        drain(ag.at[:, :, group_head(tme)], f_ss.at[m // 2])
    for c in range(chunks):
        out_copy(c).wait()


def shards(
    queries, keys, values, mem_keys, mem_values, gate_bias, out_weight, retrieved, block_slot
):
    tok, width = queries.shape
    heads = gate_bias.shape[0]
    head = width // heads
    peers = lax.axis_size("dp")
    groups = lax.axis_size("tensor")
    n = peers // 2
    local_blocks = mem_keys.shape[0] // BLOCK
    feats = out_weight.shape[1] // groups
    chunks = tok // CHUNK
    sliced = feats % 128 == 0
    weight = out_weight
    if not sliced:
        weight = out_weight.reshape(width, groups, feats).transpose(1, 0, 2)
    blocked = (local_blocks, BLOCK, width)
    bf16, f32 = jnp.bfloat16, jnp.float32
    landing = pltpu.VMEM((2 * UNIQ_CAP, BLOCK, head), bf16)
    landings = tuple(tuple(landing for _ in range(n)) for _ in range(heads))
    wide = block_slot.shape[0]
    stat_rows = 2 * CHUNK // BLOCK
    dma = pltpu.SemaphoreType.DMA
    smem = pl.BlockSpec(memory_space=pltpu.SMEM)
    any_spec = pl.BlockSpec(memory_space=pltpu.HBM)
    return pl.pallas_call(
        functools.partial(layer_kernel, n, groups, heads, peers <= 8, sliced),
        out_shape=jax.ShapeDtypeStruct((feats, tok), bf16),
        in_specs=[smem] * 3 + [any_spec] * 6,
        out_specs=pl.BlockSpec(memory_space=pl.ANY),
        scratch_shapes=[
            pltpu.VMEM((n, heads, tok, head), bf16),
            pltpu.VMEM((heads, tok, head), bf16),
            pltpu.VMEM((tok, width), bf16),
            pltpu.VMEM((heads, tok // BLOCK, head, BLOCK), bf16),
            pltpu.VMEM((heads, local_blocks, BLOCK, head), bf16),
            pltpu.VMEM(blocked, bf16),
            pltpu.VMEM((heads, local_blocks, head, BLOCK), bf16),
            pltpu.VMEM((heads, n, UNIQ_CAP, BLOCK, head), bf16),
            pltpu.VMEM((heads, n, UNIQ_CAP, head, BLOCK), bf16),
            landings,
            landings,
            pltpu.VMEM((heads, tok // BLOCK, head, BLOCK), f32),
            pltpu.VMEM((n, chunks, head, CHUNK), f32),
            pltpu.VMEM((n, chunks, stat_rows, BLOCK), f32),
            pltpu.VMEM((tok // BLOCK, TOPK * BLOCK, BLOCK), bf16),
            pltpu.VMEM((heads, n, chunks, head, CHUNK), bf16),
            pltpu.VMEM((heads, n, chunks, stat_rows, BLOCK), f32),
            pltpu.VMEM((2, n, heads, chunks, head, CHUNK), bf16),
            pltpu.VMEM((2, n, heads, chunks, stat_rows, BLOCK), f32),
            pltpu.VMEM((groups * width, feats), bf16),
            pltpu.VMEM((heads, feats, groups * head), bf16),
            pltpu.VMEM((chunks, feats, CHUNK), f32),
            pltpu.VMEM((heads, chunks, groups * head, CHUNK), bf16),
            pltpu.VMEM((chunks, feats, CHUNK), bf16),
            pltpu.VMEM((peers, 8, wide), jnp.int32),
            pltpu.SMEM((peers, 8, wide), jnp.int32),
            dma((3 * heads + 2,)),
            dma(()),
            dma(()),
            dma((chunks,)),
            dma(()),
            dma((peers,)),
            dma((2, n)),
            dma((n, heads, chunks)),
            dma(()),
            dma((heads, n)),
            dma(()),
            dma((heads, n)),
            dma(()),
            dma((2, n, heads, chunks)),
            dma(()),
            dma((2, n, heads, chunks)),
            dma((groups,)),
            dma((groups,)),
            dma((groups // 2,)),
            dma((heads, chunks, groups // 2)),
            dma((groups // 2,)),
            dma((heads, chunks, groups // 2)),
        ],
        compiler_params=pltpu.CompilerParams(
            collective_id=0, has_side_effects=True, vmem_limit_bytes=(49 if peers <= 8 else 62) * 2**20
        ),
        name="memory_layer",
    )(
        *[
            pltpu.with_memory_space_constraint(operand, pltpu.HBM)
            for operand in (
                retrieved.T, block_slot, gate_bias, queries, keys, values,
                mem_keys.reshape(blocked), mem_values.reshape(blocked), weight,
            )
        ]
    )


def solution(mesh):
    in_specs = (
        P("dp", "tensor"),
        P("dp", "tensor"),
        P("dp", "tensor"),
        P("dp", "tensor"),
        P("dp", "tensor"),
        P("tensor"),
        P("tensor", None),
        P("dp", None),
        P(),
    )
    out_specs = P("tensor", "dp")
    return jax.shard_map(shards, mesh=mesh, in_specs=in_specs, out_specs=out_specs, check_vma=False)
```
